256 devices in a mesh: strip: 16 (over x, y), tile: 16 (over z, core).
Axes of the slice: x: 4, y: 4, z: 8, core: 2. Of those that a mesh axis runs over, the one named last changes fastest.
Arguments:
- object_field: float32 [2, 2, 2048, 2048], P(None, None, 'strip', 'tile'), may hold values from -1 to 1
- probe_modes: float32 [2, 4, 256, 256], replicated, may hold values from -6 to 6
- offsets: int32 [512, 2], P(('strip', 'tile')), may hold values from 0 to 2047, as said below
- measured: float32 [512, 256, 256], P(('strip', 'tile')), may hold values from 0.5 to 6
Outputs:
- object_grad: float32 [2, 2, 2048, 2048], P(None, None, 'strip', 'tile')
- probe_grad: float32 [2, 4, 256, 256], replicated
The draws below stay inside these ranges and needn't reach their ends.
Inputs may be any that keep to these rules, and one draw needn't show every extreme that they name: `offsets`: column 0 is a window's row offset, column 1 its column offset. A window held by the device with strip index s and tile index t has its row offset between s * 128 and (s + 1) * 128 - 1 and its column offset between t * 128 and (t + 1) * 128 - 1.
All inputs are finite; a program needn't handle non-finite values.
Results may differ from the reference program's by a relative error of at most 0.0003.
Values sent between devices are 32-bit elements; how exact they have to be, the bound alone decides.
No kernel may reach another device: no remote copies, remote signals or barrier semaphores. Data moves between devices by JAX's collectives and lax.ppermute only.
A program may use at most 64 MiB of HBM per device.

```python
import math
import jax
import jax.numpy as jnp
from jax import lax

W = 256
MODES = 4
SLICES = 2
TILE = 128
POS_DEV = 2
NY = 2048
NX = 2048
NPOS = 512


def draw_offsets(key, part):
    count_all = NPOS
    counter = jnp.arange(count_all, dtype=jnp.int32)
    tiles_wide = NX // TILE
    strip_of = counter // (POS_DEV * tiles_wide)
    tile_of = counter // POS_DEV % tiles_wide
    row_key, col_key = jax.random.split(key)
    rows_drawn = strip_of * TILE + jax.random.randint(row_key, (count_all,), 0, TILE, dtype=jnp.int32)
    cols_drawn = tile_of * TILE + jax.random.randint(col_key, (count_all,), 0, TILE, dtype=jnp.int32)
    rows_drawn = jnp.where(counter == 0, 0, rows_drawn)
    rows_drawn = jnp.where(counter == count_all - 1, NY - 1, rows_drawn)
    cols_drawn = jnp.where(counter == 0, 0, cols_drawn)
    cols_drawn = jnp.where(counter == count_all - 1, NX - 1, cols_drawn)
    return jnp.stack([rows_drawn, cols_drawn], axis=1).astype(jnp.int32)


def block_levels(rng, dims, cuts, low, top_value):
    level = 1.0
    for axis_at, blocks in cuts:
        draws = jax.random.uniform(jax.random.fold_in(jax.random.fold_in(rng, 6), axis_at), (blocks,), jnp.float32, low / len(cuts), top_value / len(cuts))
        level = level * jnp.repeat(jnp.exp(draws), dims[axis_at] // blocks).reshape((-1,) + (1,) * (len(dims) - 1 - axis_at))
    return level


def gaussian(rng, shape, width, bound, kind=jnp.bfloat16):
    array = width * jax.random.normal(rng, shape, jnp.float32)
    return jnp.clip(array, min=-bound, max=bound).astype(kind)


def setup_inputs(seed: int = 0) -> dict:
    keys = jax.random.split(jax.random.key(seed), 5)
    object_field = jnp.clip(jax.random.uniform(keys[0], (2, SLICES, NY, NX), jnp.float32, -1.0, 1.0) * block_levels(keys[0], (2, SLICES, NY, NX), ((2, 16), (3, 16)), -0.4, 0.0), -1.0, 1.0)
    probe_modes = gaussian(keys[1], (2, MODES, W, W), 1.0, 6.0, jnp.float32)
    offsets = draw_offsets(jax.random.fold_in(keys[4], 71), 0)
    measured = jnp.clip(jnp.exp(math.log(6.0) - 2.4849066 * jax.random.uniform(keys[3], (NPOS, W, W), jnp.float32) ** block_levels(keys[3], (NPOS, W, W), ((0, 256),), -0.2, 0.2)), 0.5, 6.0)
    return dict(object_field=object_field, probe_modes=probe_modes, offsets=offsets, measured=measured)


TWO_PI = 6.283185307179586
FRESNEL = 0.5

def product_left(matrix, field):
    return jnp.einsum('ij,...jk->...ik', matrix, field, precision=lax.Precision.HIGHEST)

def product_right(field, matrix):
    return jnp.einsum('...ij,jk->...ik', field, matrix, precision=lax.Precision.HIGHEST)

def sandwich(matrix_re, matrix_im, field_re, field_im):
    inner_re = product_left(matrix_re, field_re) - product_left(matrix_im, field_im)
    inner_im = product_left(matrix_re, field_im) + product_left(matrix_im, field_re)
    outer_re = product_right(inner_re, matrix_re) - product_right(inner_im, matrix_im)
    outer_im = product_right(inner_re, matrix_im) + product_right(inner_im, matrix_re)
    return (outer_re, outer_im)

def make_tables(length):
    counter = jnp.arange(length, dtype=jnp.int32)
    product = counter[:, None] * counter[None, :] % length
    angles = product.astype(jnp.float32) * (TWO_PI / length)
    factor = 1.0 / math.sqrt(length)
    four_re = jnp.cos(angles) * factor
    four_im = -jnp.sin(angles) * factor
    centred = (counter + length // 2) % length - length // 2
    phases = -0.5 * TWO_PI * FRESNEL * (centred * centred).astype(jnp.float32) / length
    kernel_re = jnp.cos(phases)
    kernel_im = jnp.sin(phases)
    left_re = four_re * kernel_re[None, :] + four_im * kernel_im[None, :]
    left_im = four_re * kernel_im[None, :] - four_im * kernel_re[None, :]
    highest = lax.Precision.HIGHEST
    prop_re = jnp.dot(left_re, four_re, precision=highest) - jnp.dot(left_im, four_im, precision=highest)
    prop_im = jnp.dot(left_re, four_im, precision=highest) + jnp.dot(left_im, four_re, precision=highest)
    return (four_re, four_im, prop_re, prop_im)

def window_grads(window, probe_modes, amplitude, tables):
    four_re, four_im, prop_re, prop_im = tables
    top_re, top_im = (window[0, 0], window[1, 0])
    low_re, low_im = (window[0, 1], window[1, 1])
    probe_re, probe_im = (probe_modes[0], probe_modes[1])
    entry_re = probe_re * top_re - probe_im * top_im
    entry_im = probe_re * top_im + probe_im * top_re
    moved_re, moved_im = sandwich(prop_re, prop_im, entry_re, entry_im)
    exit_re = moved_re * low_re - moved_im * low_im
    exit_im = moved_re * low_im + moved_im * low_re
    far_re, far_im = sandwich(four_re, four_im, exit_re, exit_im)
    intensity = lax.optimization_barrier(jnp.sum(far_re * far_re + far_im * far_im, axis=0))
    scaling = 1.0 - amplitude / jnp.sqrt(intensity + 1.0)
    misfit_re = scaling * far_re
    misfit_im = scaling * far_im
    back_re, back_im = sandwich(four_re, -four_im, misfit_re, misfit_im)
    grad_low_re = lax.optimization_barrier(jnp.sum(moved_re * back_re + moved_im * back_im, axis=0))
    grad_low_im = lax.optimization_barrier(jnp.sum(moved_re * back_im - moved_im * back_re, axis=0))
    behind_re = low_re * back_re + low_im * back_im
    behind_im = low_re * back_im - low_im * back_re
    source_re, source_im = sandwich(prop_re, -prop_im, behind_re, behind_im)
    grad_top_re = lax.optimization_barrier(jnp.sum(probe_re * source_re + probe_im * source_im, axis=0))
    grad_top_im = lax.optimization_barrier(jnp.sum(probe_re * source_im - probe_im * source_re, axis=0))
    grad_probe_re = top_re * source_re + top_im * source_im
    grad_probe_im = top_re * source_im - top_im * source_re
    window_grad = jnp.stack([jnp.stack([grad_top_re, grad_low_re]), jnp.stack([grad_top_im, grad_low_im])])
    probe_grad = jnp.stack([grad_probe_re, grad_probe_im])
    return (window_grad, probe_grad)

def reference(object_field, probe_modes, offsets, measured):
    tables = make_tables(W)
    counter = jnp.arange(W, dtype=jnp.int32)

    def visit(totals, record):
        object_total, probe_total = totals
        offset_pair, amplitude = record
        rows_taken = ((offset_pair[0] + counter) % NY).astype(jnp.int32)
        cols_taken = ((offset_pair[1] + counter) % NX).astype(jnp.int32)
        window = object_field[:, :, rows_taken][:, :, :, cols_taken]
        window_grad, probe_term = window_grads(window, probe_modes, amplitude, tables)
        object_total = object_total.at[:, :, rows_taken[:, None], cols_taken[None, :]].add(window_grad)
        return ((object_total, probe_total + probe_term), None)
    initial = (jnp.zeros_like(object_field), jnp.zeros_like(probe_modes))
    (object_grad, probe_grad), unused = lax.scan(visit, initial, (offsets, measured))
    return (object_grad, probe_grad)
```

```python
import jax
import jax.numpy as jnp
import ml_dtypes
import numpy as np
from jax import lax
from jax.experimental import pallas as pl
from jax.experimental.pallas import tpu as pltpu
from jax.sharding import PartitionSpec as P

FRESNEL = 0.5
BF, F32 = jnp.bfloat16, jnp.float32


def transform_tables(length):
    counter = np.arange(length)
    angles = (counter[:, None] * counter[None, :] % length) * (2 * np.pi / length)
    four = (np.cos(angles) - 1j * np.sin(angles)) / np.sqrt(length)
    centred = (counter + length // 2) % length - length // 2
    kern = np.exp(-1j * np.pi * FRESNEL * centred * centred / length)
    prop = (np.conj(four) * kern[None, :]) @ four
    parts = []
    for matrix in (four.real, four.imag, prop.real, prop.imag):
        high = matrix.astype(np.float32).astype(ml_dtypes.bfloat16)
        low = (matrix - high.astype(np.float64)).astype(np.float32)
        parts += [high, low.astype(ml_dtypes.bfloat16)]
    return np.stack(parts)


def halves(value):
    high = value.astype(BF)
    return high, (value - high.astype(F32)).astype(BF)


def product(a_high, a_low, b_high, b_low):
    total = jnp.dot(a_high, b_high, preferred_element_type=F32)
    total = total + jnp.dot(a_low, b_high, preferred_element_type=F32)
    return total + jnp.dot(a_high, b_low, preferred_element_type=F32)


FOUR, FOUR_CONJ, PROP, PROP_CONJ = 0, 1, 2, 3


def window_kernel(
    offsets, left, middle, right, probe, measured, base,
    grad_left, grad_middle, grad_right, probe_grad,
    window, moved, far, scaling, grads, tables, wide,
):
    n = probe.shape[2]
    modes = probe.shape[1]
    rows, tile = middle.shape[2], middle.shape[3]
    count = measured.shape[0]
    wide[:, :, :, :tile] = left[...]
    wide[:, :, :, tile : 2 * tile] = middle[...]
    wide[:, :, :, 2 * tile :] = right[...]
    for field in range(2):
        for part in range(2):
            re, im = base[4 * field + part], base[4 * field + 2 + part]
            for conj in range(2):
                which = 2 * field + conj
                upper, lower = (im, -im) if conj == 0 else (-im, im)
                tables[which, part, :n, :n] = re
                tables[which, part, n:, n:] = re
                tables[which, part, :n, n:] = upper
                tables[which, part, n:, :n] = lower

    def sandwich(re, im, which):
        re_high, re_low = halves(re)
        im_high, im_low = halves(im)
        inner = product(
            jnp.concatenate([re_high, im_high], axis=1),
            jnp.concatenate([re_low, im_low], axis=1),
            tables[which, 0],
            tables[which, 1],
        )
        re_high, re_low = halves(inner[:, :n])
        im_high, im_low = halves(inner[:, n:])
        outer = product(
            tables[which ^ 1, 0],
            tables[which ^ 1, 1],
            jnp.concatenate([re_high, im_high], axis=0),
            jnp.concatenate([re_low, im_low], axis=0),
        )
        return outer[:n], outer[n:]

    probe_grad[...] = jnp.zeros_like(probe_grad)

    def visit(position, carry):
        row, col = offsets[position, 0], offsets[position, 1]
        for part in range(2):
            for layer in range(2):
                plane = pltpu.roll(wide[part, layer], 3 * tile - col, 1)[:, :n]
                window[part, layer] = pltpu.roll(plane, rows - row, 0)[:n]
        scaling[...] = jnp.zeros_like(scaling)

        def forward(mode, carry):
            probe_re, probe_im = probe[0, mode], probe[1, mode]
            top_re, top_im = window[0, 0], window[1, 0]
            moved_re, moved_im = sandwich(
                probe_re * top_re - probe_im * top_im,
                probe_re * top_im + probe_im * top_re,
                PROP,
            )
            moved[0, mode] = moved_re
            moved[1, mode] = moved_im
            low_re, low_im = window[0, 1], window[1, 1]
            far_re, far_im = sandwich(
                moved_re * low_re - moved_im * low_im,
                moved_re * low_im + moved_im * low_re,
                FOUR,
            )
            far[0, mode] = far_re
            far[1, mode] = far_im
            scaling[...] += far_re * far_re + far_im * far_im
            return carry

        lax.fori_loop(0, modes, forward, 0)
        scaling[...] = 1.0 - measured[position] / jnp.sqrt(scaling[...] + 1.0)
        grads[...] = jnp.zeros_like(grads)

        def backward(mode, carry):
            factor = scaling[...]
            back_re, back_im = sandwich(factor * far[0, mode], factor * far[1, mode], FOUR_CONJ)
            moved_re, moved_im = moved[0, mode], moved[1, mode]
            grads[0, 1] += moved_re * back_re + moved_im * back_im
            grads[1, 1] += moved_re * back_im - moved_im * back_re
            low_re, low_im = window[0, 1], window[1, 1]
            source_re, source_im = sandwich(
                low_re * back_re + low_im * back_im,
                low_re * back_im - low_im * back_re,
                PROP_CONJ,
            )
            probe_re, probe_im = probe[0, mode], probe[1, mode]
            grads[0, 0] += probe_re * source_re + probe_im * source_im
            grads[1, 0] += probe_re * source_im - probe_im * source_re
            top_re, top_im = window[0, 0], window[1, 0]
            probe_grad[0, mode] += top_re * source_re + top_im * source_im
            probe_grad[1, mode] += top_re * source_im - top_im * source_re
            return carry

        lax.fori_loop(0, modes, backward, 0)
        for part in range(2):
            for layer in range(2):
                plane = jnp.concatenate(
                    [grads[part, layer], jnp.zeros((rows - n, n), F32)], axis=0
                )
                plane = pltpu.roll(plane, row, 0)
                plane = jnp.concatenate(
                    [plane, jnp.zeros((rows, 3 * tile - n), F32)], axis=1
                )
                plane = pltpu.roll(plane, col, 1)
                for at, target in enumerate((grad_left, grad_middle, grad_right)):
                    piece = plane[:, at * tile : (at + 1) * tile]

                    @pl.when(position == 0)
                    def _():
                        target[part, layer] = piece

                    @pl.when(position != 0)
                    def _():
                        target[part, layer] += piece

        return carry

    lax.fori_loop(0, count, visit, 0)


def window_gradients(offsets, left, middle, right, probe, measured):
    n, modes = probe.shape[2], probe.shape[1]
    rows, tile = middle.shape[2], middle.shape[3]
    base = jnp.asarray(transform_tables(n))
    vmem = pl.BlockSpec(memory_space=pltpu.VMEM)
    column = jax.ShapeDtypeStruct(middle.shape, F32)
    products = 2 * measured.shape[0] * modes * 4 * 2 * 4 * 3 * n**3
    return pl.pallas_call(
        window_kernel,
        out_shape=(column, column, column, jax.ShapeDtypeStruct(probe.shape, F32)),
        in_specs=[pl.BlockSpec(memory_space=pltpu.SMEM)] + [vmem] * 6,
        out_specs=(vmem,) * 4,
        scratch_shapes=[
            pltpu.VMEM((2, 2, n, n), F32),
            pltpu.VMEM(probe.shape, F32),
            pltpu.VMEM(probe.shape, F32),
            pltpu.VMEM((n, n), F32),
            pltpu.VMEM((2, 2, n, n), F32),
            pltpu.VMEM((4, 2, 2 * n, 2 * n), BF),
            pltpu.VMEM((2, 2, rows, 3 * tile), F32),
        ],
        compiler_params=pltpu.CompilerParams(vmem_limit_bytes=32 << 20),
        cost_estimate=pl.CostEstimate(flops=products, bytes_accessed=12 << 20, transcendentals=n * n),
        name="window_gradients",
    )(offsets, left, middle, right, probe, measured, base)


def around(value, axis, steps):
    count = lax.axis_size(axis)
    return lax.ppermute(value, axis, [(at, (at + steps) % count) for at in range(count)])


def exchanged(value, axis, groups=None):
    return lax.all_to_all(value, axis, 0, 0, tiled=True, axis_index_groups=groups)


def copies(value, count):
    return jnp.broadcast_to(value[None], (count,) + value.shape)


def paired_half(value):
    tiles = lax.axis_size("tile")
    core = lax.axis_index("tile") % 2
    kept = lax.dynamic_index_in_dim(value, core, 0, False)
    sent = lax.dynamic_index_in_dim(value, 1 - core, 0, False)
    return kept + lax.ppermute(sent, "tile", [(at, at ^ 1) for at in range(tiles)])


def paired_whole(half):
    tiles = lax.axis_size("tile")
    first = lax.axis_index("tile") % 2 == 0
    other = lax.ppermute(half, "tile", [(at, at ^ 1) for at in range(tiles)])
    return jnp.stack([jnp.where(first, half, other), jnp.where(first, other, half)])


def per_device(object_field, probe_modes, offsets, measured):
    tile = object_field.shape[2]
    strips, tiles = lax.axis_size("strip"), lax.axis_size("tile")
    local = jnp.stack(
        [
            (offsets[:, 0] - lax.axis_index("strip") * tile) % (tile * strips),
            (offsets[:, 1] - lax.axis_index("tile") * tile) % (tile * tiles),
        ],
        axis=1,
    )
    diagonal = [
        (s * tiles + t, (s + 1) % strips * tiles + (t + 1) % tiles)
        for s in range(strips)
        for t in range(tiles)
    ]
    above = around(object_field, "strip", 1)
    below = around(object_field, "strip", -1)
    middle = jnp.concatenate([above, object_field, below], axis=2)
    left = around(middle, "tile", 1)
    right = around(middle, "tile", -1)
    moved_offsets = lax.ppermute(local, ("strip", "tile"), diagonal)
    moved_measured = lax.ppermute(measured, ("strip", "tile"), diagonal)
    grad_left, grad_middle, grad_right, grad_probe = window_gradients(
        moved_offsets, left, middle, right, probe_modes, moved_measured
    )
    levels = [[core + 2 * z for z in range(tiles // 2)] for core in range(2)]
    from_right = around(grad_left, "tile", -1)
    from_left = around(grad_right, "tile", 1)
    part = paired_half(grad_probe.reshape(2, strips, -1, grad_probe.shape[-1]))
    shares = exchanged(part, "strip")
    shares, from_right, from_left = lax.optimization_barrier((shares, from_right, from_left))
    column = grad_middle + from_right + from_left
    from_below = around(column[:, :, :tile], "strip", -1)
    from_above = around(column[:, :, 2 * tile :], "strip", 1)
    shares = exchanged(copies(jnp.sum(shares, axis=0), tiles // 2), "tile", levels)
    shares, from_below, from_above = lax.optimization_barrier((shares, from_below, from_above))
    object_grad = column[:, :, tile : 2 * tile] + from_below + from_above
    half = exchanged(copies(jnp.sum(shares, axis=0), strips), "strip")
    return (object_grad, paired_whole(half).reshape(grad_probe.shape))


def solution(mesh):
    in_specs = (
        P(None, None, "strip", "tile"),
        P(),
        P(("strip", "tile"), None),
        P(("strip", "tile"), None, None),
    )
    out_specs = (P(None, None, "strip", "tile"), P())
    return jax.shard_map(
        per_device, mesh=mesh, in_specs=in_specs, out_specs=out_specs, check_vma=False
    )
```

```python
import jax
import jax.numpy as jnp
import ml_dtypes
import numpy as np
from jax import lax
from jax.experimental import pallas as pl
from jax.experimental.pallas import tpu as pltpu
from jax.sharding import PartitionSpec as P

FRESNEL = 0.5
BF, F32 = jnp.bfloat16, jnp.float32
FOUR, FOUR_CONJ, PROP, PROP_CONJ = 0, 1, 2, 3
VMEM = pl.BlockSpec(memory_space=pltpu.VMEM)
SMEM = pl.BlockSpec(memory_space=pltpu.SMEM)
ANY = pl.BlockSpec(memory_space=pl.ANY)
HBM = pl.BlockSpec(memory_space=pltpu.HBM)


def parity_tables(length):
    half = length // 2
    counter = np.arange(length)
    angles = (counter[:, None] * counter[None, :] % length) * (2 * np.pi / length)
    four = np.exp(-1j * angles) / np.sqrt(length)
    mirrored = np.concatenate([counter[:half], counter[:half - 1:-1]])
    quarter = counter - (length - 1) / 2
    shifted = np.exp(-2j * np.pi * quarter[:, None] * quarter[None, :] / length) / np.sqrt(length)
    centred = (counter + half) % length - half
    kern = np.exp(-1j * np.pi * FRESNEL * centred * centred / length)
    prop = (np.conj(four) * kern[None, :]) @ four
    blocks = []
    for matrix in (shifted, prop):
        folded = matrix[mirrored][:, mirrored]
        same, cross = folded[:half, :half], folded[:half, half:]
        even, odd = (same + cross) / 2, (same - cross) / 2
        for part in ("real", "imag"):
            for block in (even, odd):
                value = getattr(block, part)
                high = value.astype(np.float32).astype(ml_dtypes.bfloat16)
                low = (value - high.astype(np.float64)).astype(np.float32)
                blocks += [high, low.astype(ml_dtypes.bfloat16)]
    turn = np.exp(-2j * np.pi * ((length - 1) / 2) * counter / length)[mirrored]
    phase = turn[:, None] * turn[None, :]
    phase = np.stack([phase.real, phase.imag]).astype(np.float32)
    return np.stack(blocks).reshape(2, 2, 2, 2, half, half), phase


def halves(value):
    high = value.astype(BF)
    return high, (value - high.astype(F32)).astype(BF)


def product(a_high, a_low, b_high, b_low):
    total = jnp.dot(a_high, b_high, preferred_element_type=F32)
    total = total + jnp.dot(a_low, b_high, preferred_element_type=F32)
    return total + jnp.dot(a_high, b_low, preferred_element_type=F32)


def anti_diagonal(h):
    row_at = lax.broadcasted_iota(jnp.int32, (h, h), 0)
    col_at = lax.broadcasted_iota(jnp.int32, (h, h), 1)
    return (row_at + col_at == h - 1).astype(F32).astype(BF)


def folded(planes):
    n = planes[0].shape[0]
    h = n // 2
    anti = anti_diagonal(h)
    flipped = jnp.dot(
        jnp.concatenate([jnp.concatenate(halves(plane[:, h:]), axis=1) for plane in planes], axis=0),
        jnp.concatenate([anti, anti], axis=0),
        preferred_element_type=F32,
    )
    planes = [
        jnp.concatenate([plane[:, :h], flipped[at * n : (at + 1) * n]], axis=1)
        for at, plane in enumerate(planes)
    ]
    flipped = jnp.dot(
        jnp.concatenate([anti, anti], axis=1),
        jnp.concatenate([jnp.concatenate(halves(plane[h:]), axis=0) for plane in planes], axis=1),
        preferred_element_type=F32,
    )
    return [
        jnp.concatenate([plane[:h], flipped[:, at * n : (at + 1) * n]], axis=0)
        for at, plane in enumerate(planes)
    ]


def sandwich(fields, which, tables, lhs_high, lhs_low, rhs_high, rhs_low):
    n = tables.shape[-1]
    h = n // 2
    for at, field in enumerate(fields):
        for part in range(2):
            first, second = field[part][:, :h], field[part][:, h:]
            for parity, value in enumerate((first + second, first - second)):
                high, low = halves(value)
                lhs_high[parity, at * n : (at + 1) * n, part * h : (part + 1) * h] = high
                lhs_low[parity, at * n : (at + 1) * n, part * h : (part + 1) * h] = low
    for parity in range(2):
        inner = product(
            lhs_high[parity], lhs_low[parity], tables[which, parity, 0], tables[which, parity, 1]
        )
        for at in range(len(fields)):
            first = inner[at * n : at * n + h]
            second = inner[at * n + h : (at + 1) * n]
            cols = slice(at * n + parity * h, at * n + (parity + 1) * h)
            for turned, value in enumerate((first + second, first - second)):
                high, low = halves(value)
                rhs_high[turned, :h, cols] = high[:, :h]
                rhs_high[turned, h:, cols] = high[:, h:]
                rhs_low[turned, :h, cols] = low[:, :h]
                rhs_low[turned, h:, cols] = low[:, h:]
    even, odd = [
        product(
            tables[which ^ 1, turned, 0], tables[which ^ 1, turned, 1],
            rhs_high[turned], rhs_low[turned],
        )
        for turned in range(2)
    ]
    results = []
    for at in range(len(fields)):
        pair = []
        for part in range(2):
            e = even[part * h : (part + 1) * h, at * n : (at + 1) * n]
            o = odd[part * h : (part + 1) * h, at * n : (at + 1) * n]
            value = jnp.concatenate([e + o, e - o], axis=0)
            first, second = value[:, :h], value[:, h:]
            pair.append(jnp.concatenate([first + second, first - second], axis=1))
        results.append(pair)
    return results


def sandwich_scratch(n, modes):
    return [
        pltpu.VMEM((2, modes * n, n), BF),
        pltpu.VMEM((2, modes * n, n), BF),
        pltpu.VMEM((2, n, modes * n), BF),
        pltpu.VMEM((2, n, modes * n), BF),
    ]


def prepare_kernel(probe_in, measured_in, blocks, probe, measured, tables):
    h = blocks.shape[-1]
    for field in range(2):
        for parity in range(2):
            for part in range(2):
                re, im = blocks[field, 0, parity, part], blocks[field, 1, parity, part]
                for conj in range(2):
                    which = 2 * field + conj
                    upper, lower = (im, -im) if conj == 0 else (-im, im)
                    tables[which, parity, part, :h, :h] = re
                    tables[which, parity, part, h:, h:] = re
                    tables[which, parity, part, :h, h:] = upper
                    tables[which, parity, part, h:, :h] = lower

    def fold(part, carry):
        planes = folded([probe_in[part, mode] for mode in range(probe.shape[1])])
        for mode, plane in enumerate(planes):
            probe[part, mode] = plane
        return carry

    lax.fori_loop(0, 2, fold, 0)
    for at, plane in enumerate(folded([measured_in[at] for at in range(measured.shape[0])])):
        measured[at] = plane


def prepared(probe, measured, blocks):
    n = probe.shape[-1]
    return pl.pallas_call(
        prepare_kernel,
        out_shape=(
            jax.ShapeDtypeStruct(probe.shape, F32),
            jax.ShapeDtypeStruct(measured.shape, F32),
            jax.ShapeDtypeStruct((4, 2, 2, n, n), BF),
        ),
        in_specs=[VMEM] * 3,
        out_specs=(VMEM,) * 3,
        compiler_params=pltpu.CompilerParams(vmem_limit_bytes=24 << 20),
        cost_estimate=pl.CostEstimate(flops=3 << 30, bytes_accessed=6 << 20, transcendentals=0),
        name="prepare",
    )(probe, measured, blocks)


def forward_kernel(
    offsets, left, middle, right, probe, tables, phase,
    window, moved, far, intensity,
    lhs_high, lhs_low, rhs_high, rhs_low, wide, sems,
):
    n, modes = probe.shape[-1], probe.shape[1]
    rows, tile = wide.shape[2], wide.shape[3] // 3
    columns = [
        pltpu.make_async_copy(source, wide.at[:, :, :, at * tile : (at + 1) * tile], sems.at[at])
        for at, source in enumerate((left, middle, right))
    ]
    for column in columns:
        column.start()
    for column in columns:
        column.wait()
    buffers = (tables, lhs_high, lhs_low, rhs_high, rhs_low)

    def visit(position, carry):
        row, col = offsets[position, 0], offsets[position, 1]
        planes = []
        for layer in range(2):
            for part in range(2):
                plane = pltpu.roll(wide[part, layer], 3 * tile - col, 1)[:, :n]
                planes.append(pltpu.roll(plane, rows - row, 0)[:n])
        planes = folded(planes)
        window[position, 0, 0], window[position, 1, 0] = planes[0], planes[1]
        window[position, 0, 1] = planes[2] * phase[0] - planes[3] * phase[1]
        window[position, 1, 1] = planes[2] * phase[1] + planes[3] * phase[0]
        top_re, top_im = window[position, 0, 0], window[position, 1, 0]
        fields = []
        for mode in range(modes):
            probe_re, probe_im = probe[0, mode], probe[1, mode]
            fields.append(
                (probe_re * top_re - probe_im * top_im, probe_re * top_im + probe_im * top_re)
            )
        fields = sandwich(fields, PROP, *buffers)
        low_re, low_im = window[position, 0, 1], window[position, 1, 1]
        exits = []
        for mode, (re, im) in enumerate(fields):
            moved[position, 0, mode] = re
            moved[position, 1, mode] = im
            exits.append((re * low_re - im * low_im, re * low_im + im * low_re))
        fields = sandwich(exits, FOUR, *buffers)
        total = jnp.zeros((n, n), F32)
        for mode, (re, im) in enumerate(fields):
            far[position, 0, mode] = re
            far[position, 1, mode] = im
            total = total + (re * re + im * im)
        intensity[position] = total
        return carry

    lax.fori_loop(0, window.shape[0], visit, 0)


def forward(count, offsets, left, middle, right, probe, tables, phase):
    n, modes = probe.shape[-1], probe.shape[1]
    rows, tile = middle.shape[2], middle.shape[3]
    fields = jax.ShapeDtypeStruct((count,) + probe.shape, F32)
    return pl.pallas_call(
        forward_kernel,
        out_shape=(
            jax.ShapeDtypeStruct((count, 2, 2, n, n), F32),
            fields,
            fields,
            jax.ShapeDtypeStruct((count, n, n), F32),
        ),
        in_specs=[SMEM] + [ANY] * 3 + [VMEM] * 3,
        out_specs=(VMEM,) * 4,
        scratch_shapes=sandwich_scratch(n, modes)
        + [pltpu.VMEM((2, 2, rows, 3 * tile), F32), pltpu.SemaphoreType.DMA((3,))],
        compiler_params=pltpu.CompilerParams(vmem_limit_bytes=SCOPED_F << 20),
        cost_estimate=pl.CostEstimate(
            flops=count * modes * 8 * 12 * n**3, bytes_accessed=18 << 20, transcendentals=0
        ),
        name="forward",
    )(offsets, left, middle, right, probe, tables, phase)


def backward_kernel(
    scalars, window, moved, far, intensity, measured, probe, tables, phase,
    grad_left, grad_middle, grad_right, kept, sent,
    lhs_high, lhs_low, rhs_high, rhs_low, wide, probe_grad, sems,
):
    n, modes = probe.shape[-1], probe.shape[1]
    rows, tile = wide.shape[2], wide.shape[3] // 3
    count = window.shape[0]
    buffers = (tables, lhs_high, lhs_low, rhs_high, rhs_low)

    def visit(position, carry):
        scaling = 1.0 - measured[position] / jnp.sqrt(intensity[position] + 1.0)
        fields = [
            (scaling * far[position, 0, mode], scaling * far[position, 1, mode])
            for mode in range(modes)
        ]
        fields = sandwich(fields, FOUR_CONJ, *buffers)
        low_re, low_im = window[position, 0, 1], window[position, 1, 1]
        total_re = total_im = jnp.zeros((n, n), F32)
        behinds = []
        for mode, (re, im) in enumerate(fields):
            moved_re, moved_im = moved[position, 0, mode], moved[position, 1, mode]
            total_re = total_re + (moved_re * re + moved_im * im)
            total_im = total_im + (moved_re * im - moved_im * re)
            behinds.append((low_re * re + low_im * im, low_re * im - low_im * re))
        grad_low = (
            total_re * phase[0] + total_im * phase[1],
            total_im * phase[0] - total_re * phase[1],
        )
        fields = sandwich(behinds, PROP_CONJ, *buffers)
        top_re, top_im = window[position, 0, 0], window[position, 1, 0]
        total_re = total_im = jnp.zeros((n, n), F32)
        for mode, (re, im) in enumerate(fields):
            probe_re, probe_im = probe[0, mode], probe[1, mode]
            total_re = total_re + (probe_re * re + probe_im * im)
            total_im = total_im + (probe_re * im - probe_im * re)
            term_re = top_re * re + top_im * im
            term_im = top_re * im - top_im * re

            @pl.when(position == 0)
            def _():
                probe_grad[0, mode] = term_re
                probe_grad[1, mode] = term_im

            @pl.when(position != 0)
            def _():
                probe_grad[0, mode] += term_re
                probe_grad[1, mode] += term_im

        planes = folded([total_re, total_im, *grad_low])
        row, col = scalars[position, 0], scalars[position, 1]
        for layer in range(2):
            for part in range(2):
                plane = jnp.concatenate(
                    [planes[2 * layer + part], jnp.zeros((rows - n, n), F32)], axis=0
                )
                plane = pltpu.roll(plane, row, 0)
                plane = jnp.concatenate([plane, jnp.zeros((rows, 3 * tile - n), F32)], axis=1)
                plane = pltpu.roll(plane, col, 1)

                @pl.when(position == 0)
                def _():
                    wide[part, layer] = plane

                @pl.when(position != 0)
                def _():
                    wide[part, layer] += plane

        return carry

    lax.fori_loop(0, count, visit, 0)
    copies = [
        pltpu.make_async_copy(wide.at[:, :, :, at * tile : (at + 1) * tile], target, sems.at[at])
        for at, target in enumerate((grad_left, grad_middle, grad_right))
    ]
    for copy in copies:
        copy.start()

    def unfold(part, carry):
        planes = folded([probe_grad[part, mode] for mode in range(modes)])
        for mode in range(modes):
            probe_grad[part, mode] = planes[mode]
        return carry

    lax.fori_loop(0, 2, unfold, 0)
    core = scalars[count, 0]
    parts = [
        pltpu.make_async_copy(probe_grad.at[core], kept, sems.at[3]),
        pltpu.make_async_copy(probe_grad.at[1 - core], sent, sems.at[4]),
    ]
    for part in parts:
        part.start()
    for copy in copies + parts:
        copy.wait()


def backward(scalars, state, measured, probe, tables, phase, rows, tile):
    n, modes = probe.shape[-1], probe.shape[1]
    count = measured.shape[0]
    column = jax.ShapeDtypeStruct((2, 2, rows, tile), F32)
    half = jax.ShapeDtypeStruct(probe.shape[1:], F32)
    return pl.pallas_call(
        backward_kernel,
        out_shape=(column, column, column, half, half),
        in_specs=[SMEM] + [VMEM] * 8,
        out_specs=(HBM,) * 5,
        scratch_shapes=sandwich_scratch(n, modes)
        + [
            pltpu.VMEM((2, 2, rows, 3 * tile), F32),
            pltpu.VMEM(probe.shape, F32),
            pltpu.SemaphoreType.DMA((5,)),
        ],
        compiler_params=pltpu.CompilerParams(vmem_limit_bytes=SCOPED_B << 20),
        cost_estimate=pl.CostEstimate(
            flops=count * modes * 8 * 12 * n**3, bytes_accessed=18 << 20, transcendentals=count * n * n
        ),
        name="backward",
    )(scalars, *state, measured, probe, tables, phase)


SCOPED_F, SCOPED_B = 20, 20


def around(value, axis, steps):
    count = lax.axis_size(axis)
    return lax.ppermute(value, axis, [(at, (at + steps) % count) for at in range(count)])


def exchanged(value, axis, groups=None):
    return lax.all_to_all(value, axis, 0, 0, tiled=True, axis_index_groups=groups)


def copies(value, count):
    return jnp.broadcast_to(value[None], (count,) + value.shape)


def swapped(value):
    return lax.ppermute(value, "tile", [(at, at ^ 1) for at in range(lax.axis_size("tile"))])


def per_device(object_field, probe_modes, offsets, measured):
    n = probe_modes.shape[-1]
    tile = object_field.shape[2]
    strips, tiles = lax.axis_size("strip"), lax.axis_size("tile")
    blocks, phase = parity_tables(n)
    phase = jnp.asarray(phase)
    diagonal = [
        (s * tiles + t, (s + 1) % strips * tiles + (t + 1) % tiles)
        for s in range(strips)
        for t in range(tiles)
    ]
    corner = jnp.stack([lax.axis_index("strip"), lax.axis_index("tile")]).astype(jnp.int32) * tile
    wrap = jnp.array([strips * tile, tiles * tile], jnp.int32)
    core_there = 1 - lax.axis_index("tile") % 2
    scalars = jnp.concatenate(
        [(offsets - corner) % wrap, jnp.full((1, 2), core_there, jnp.int32)], axis=0
    )
    above = around(object_field, "strip", 1)
    below = around(object_field, "strip", -1)
    scalars = lax.ppermute(scalars, ("strip", "tile"), diagonal)
    probe, measured, tables = prepared(probe_modes, measured, jnp.asarray(blocks))
    middle = jnp.concatenate([above, object_field, below], axis=2)
    left = around(middle, "tile", 1)
    right = around(middle, "tile", -1)
    left, right, measured = lax.optimization_barrier((left, right, measured))
    measured = lax.ppermute(measured, ("strip", "tile"), diagonal)
    state = forward(measured.shape[0], scalars, left, middle, right, probe, tables, phase)
    grad_left, grad_middle, grad_right, kept, sent = backward(
        scalars, state, measured, probe, tables, phase, 3 * tile, tile
    )

    from_right = around(grad_left, "tile", -1)
    from_left = around(grad_right, "tile", 1)
    part = (kept + swapped(sent)).reshape(strips, -1, n)
    shares = exchanged(part, "strip")
    shares, from_right, from_left = lax.optimization_barrier((shares, from_right, from_left))
    column = grad_middle + from_right + from_left
    levels = [[core + 2 * z for z in range(tiles // 2)] for core in range(2)]
    share = jnp.sum(exchanged(copies(jnp.sum(shares, axis=0), tiles // 2), "tile", levels), axis=0)
    from_below = around(column[:, :, :tile], "strip", -1)
    from_above = around(column[:, :, 2 * tile :], "strip", 1)
    half = exchanged(copies(share, strips), "strip")
    half, from_below, from_above = lax.optimization_barrier((half, from_below, from_above))
    object_grad = column[:, :, tile : 2 * tile] + from_below + from_above
    other = swapped(half)
    first = lax.axis_index("tile") % 2 == 0
    whole = jnp.stack([jnp.where(first, half, other), jnp.where(first, other, half)])
    return (object_grad, whole.reshape(probe_modes.shape))


def solution(mesh):
    in_specs = (
        P(None, None, "strip", "tile"),
        P(),
        P(("strip", "tile"), None),
        P(("strip", "tile"), None, None),
    )
    out_specs = (P(None, None, "strip", "tile"), P())
    return jax.shard_map(
        per_device, mesh=mesh, in_specs=in_specs, out_specs=out_specs, check_vma=False
    )
```

```python
import jax
import jax.numpy as jnp
import ml_dtypes
import numpy as np
from jax import lax
from jax.experimental import pallas as pl
from jax.experimental.pallas import tpu as pltpu
from jax.sharding import PartitionSpec as P

FRESNEL = 0.5
BF, F32 = jnp.bfloat16, jnp.float32
FOUR, FOUR_CONJ, PROP, PROP_CONJ = 0, 1, 2, 3
VMEM = pl.BlockSpec(memory_space=pltpu.VMEM)
SMEM = pl.BlockSpec(memory_space=pltpu.SMEM)
ANY = pl.BlockSpec(memory_space=pl.ANY)
HBM = pl.BlockSpec(memory_space=pltpu.HBM)


def parity_tables(length):
    half = length // 2
    counter = np.arange(length)
    angles = (counter[:, None] * counter[None, :] % length) * (2 * np.pi / length)
    four = np.exp(-1j * angles) / np.sqrt(length)
    mirrored = np.concatenate([counter[:half], counter[:half - 1:-1]])
    quarter = counter - (length - 1) / 2
    shifted = np.exp(-2j * np.pi * quarter[:, None] * quarter[None, :] / length) / np.sqrt(length)
    centred = (counter + half) % length - half
    kern = np.exp(-1j * np.pi * FRESNEL * centred * centred / length)
    prop = (np.conj(four) * kern[None, :]) @ four
    blocks = []
    for matrix in (shifted, prop):
        folded = matrix[mirrored][:, mirrored]
        same, cross = folded[:half, :half], folded[:half, half:]
        even, odd = (same + cross) / 2, (same - cross) / 2
        for part in ("real", "imag"):
            for block in (even, odd):
                value = getattr(block, part)
                high = value.astype(np.float32).astype(ml_dtypes.bfloat16)
                low = (value - high.astype(np.float64)).astype(np.float32)
                blocks += [high, low.astype(ml_dtypes.bfloat16)]
    turn = np.exp(-2j * np.pi * ((length - 1) / 2) * counter / length)[mirrored]
    phase = turn[:, None] * turn[None, :]
    phase = np.stack([phase.real, phase.imag]).astype(np.float32)
    return np.stack(blocks).reshape(2, 2, 2, 2, half, half), phase


def halves(value):
    high = value.astype(BF)
    return high, (value - high.astype(F32)).astype(BF)


def product(a_high, a_low, b_high, b_low):
    total = jnp.dot(a_high, b_high, preferred_element_type=F32)
    total = total + jnp.dot(a_low, b_high, preferred_element_type=F32)
    return total + jnp.dot(a_high, b_low, preferred_element_type=F32)


def anti_diagonal(h):
    row_at = lax.broadcasted_iota(jnp.int32, (h, h), 0)
    col_at = lax.broadcasted_iota(jnp.int32, (h, h), 1)
    return (row_at + col_at == h - 1).astype(F32).astype(BF)


def folded(planes):
    n = planes[0].shape[0]
    h = n // 2
    anti = anti_diagonal(h)
    flipped = jnp.dot(
        jnp.concatenate([jnp.concatenate(halves(plane[:, h:]), axis=1) for plane in planes], axis=0),
        jnp.concatenate([anti, anti], axis=0),
        preferred_element_type=F32,
    )
    planes = [
        jnp.concatenate([plane[:, :h], flipped[at * n : (at + 1) * n]], axis=1)
        for at, plane in enumerate(planes)
    ]
    flipped = jnp.dot(
        jnp.concatenate([anti, anti], axis=1),
        jnp.concatenate([jnp.concatenate(halves(plane[h:]), axis=0) for plane in planes], axis=1),
        preferred_element_type=F32,
    )
    return [
        jnp.concatenate([plane[:h], flipped[:, at * n : (at + 1) * n]], axis=0)
        for at, plane in enumerate(planes)
    ]


def sandwich(fields, which, tables, lhs_high, lhs_low, rhs_high, rhs_low):
    n = tables.shape[-1]
    h = n // 2
    for at, field in enumerate(fields):
        for part in range(2):
            first, second = field[part][:, :h], field[part][:, h:]
            for parity, value in enumerate((first + second, first - second)):
                high, low = halves(value)
                lhs_high[parity, at * n : (at + 1) * n, part * h : (part + 1) * h] = high
                lhs_low[parity, at * n : (at + 1) * n, part * h : (part + 1) * h] = low
    for parity in range(2):
        inner = product(
            lhs_high[parity], lhs_low[parity], tables[which, parity, 0], tables[which, parity, 1]
        )
        for at in range(len(fields)):
            first = inner[at * n : at * n + h]
            second = inner[at * n + h : (at + 1) * n]
            cols = slice(at * n + parity * h, at * n + (parity + 1) * h)
            for turned, value in enumerate((first + second, first - second)):
                high, low = halves(value)
                rhs_high[turned, :h, cols] = high[:, :h]
                rhs_high[turned, h:, cols] = high[:, h:]
                rhs_low[turned, :h, cols] = low[:, :h]
                rhs_low[turned, h:, cols] = low[:, h:]
    even, odd = [
        product(
            tables[which ^ 1, turned, 0], tables[which ^ 1, turned, 1],
            rhs_high[turned], rhs_low[turned],
        )
        for turned in range(2)
    ]
    results = []
    for at in range(len(fields)):
        pair = []
        for part in range(2):
            e = even[part * h : (part + 1) * h, at * n : (at + 1) * n]
            o = odd[part * h : (part + 1) * h, at * n : (at + 1) * n]
            value = jnp.concatenate([e + o, e - o], axis=0)
            first, second = value[:, :h], value[:, h:]
            pair.append(jnp.concatenate([first + second, first - second], axis=1))
        results.append(pair)
    return results


def sandwich_scratch(n, modes):
    return [
        pltpu.VMEM((2, modes * n, n), BF),
        pltpu.VMEM((2, modes * n, n), BF),
        pltpu.VMEM((2, n, modes * n), BF),
        pltpu.VMEM((2, n, modes * n), BF),
    ]


def prepare_kernel(probe_in, blocks, probe, tables):
    h = blocks.shape[-1]
    for field in range(2):
        for parity in range(2):
            for part in range(2):
                re, im = blocks[field, 0, parity, part], blocks[field, 1, parity, part]
                for conj in range(2):
                    which = 2 * field + conj
                    upper, lower = (im, -im) if conj == 0 else (-im, im)
                    tables[which, parity, part, :h, :h] = re
                    tables[which, parity, part, h:, h:] = re
                    tables[which, parity, part, :h, h:] = upper
                    tables[which, parity, part, h:, :h] = lower

    def fold(part, carry):
        planes = folded([probe_in[part, mode] for mode in range(probe.shape[1])])
        for mode, plane in enumerate(planes):
            probe[part, mode] = plane
        return carry

    lax.fori_loop(0, 2, fold, 0)


def prepared(probe, blocks):
    n = probe.shape[-1]
    return pl.pallas_call(
        prepare_kernel,
        out_shape=(
            jax.ShapeDtypeStruct(probe.shape, F32),
            jax.ShapeDtypeStruct((4, 2, 2, n, n), BF),
        ),
        in_specs=[VMEM] * 2,
        out_specs=(VMEM,) * 2,
        compiler_params=pltpu.CompilerParams(vmem_limit_bytes=24 << 20),
        cost_estimate=pl.CostEstimate(flops=3 << 30, bytes_accessed=6 << 20, transcendentals=0),
        name="prepare",
    )(probe, blocks)


def forward_kernel(
    offsets, left, left_edges, middle, middle_edges, right, right_edges, probe, tables, phase,
    window, moved, far, intensity,
    lhs_high, lhs_low, rhs_high, rhs_low, wide, sems,
):
    n, modes = probe.shape[-1], probe.shape[1]
    rows, tile = wide.shape[2], wide.shape[3] // 3
    pieces = []
    for across, (own, edges) in enumerate(
        ((left, left_edges), (middle, middle_edges), (right, right_edges))
    ):
        sources = (edges.at[:, :, :tile], own, edges.at[:, :, tile:])
        for down, source in enumerate(sources):
            place = wide.at[
                :, :, down * tile : (down + 1) * tile, across * tile : (across + 1) * tile
            ]
            pieces.append(pltpu.make_async_copy(source, place, sems.at[len(pieces)]))
    for piece in pieces:
        piece.start()
    for piece in pieces:
        piece.wait()
    buffers = (tables, lhs_high, lhs_low, rhs_high, rhs_low)

    def visit(position, carry):
        row, col = offsets[position, 0], offsets[position, 1]
        planes = []
        for layer in range(2):
            for part in range(2):
                plane = pltpu.roll(wide[part, layer], 3 * tile - col, 1)[:, :n]
                planes.append(pltpu.roll(plane, rows - row, 0)[:n])
        planes = folded(planes)
        window[position, 0, 0], window[position, 1, 0] = planes[0], planes[1]
        window[position, 0, 1] = planes[2] * phase[0] - planes[3] * phase[1]
        window[position, 1, 1] = planes[2] * phase[1] + planes[3] * phase[0]
        top_re, top_im = window[position, 0, 0], window[position, 1, 0]
        fields = []
        for mode in range(modes):
            probe_re, probe_im = probe[0, mode], probe[1, mode]
            fields.append(
                (probe_re * top_re - probe_im * top_im, probe_re * top_im + probe_im * top_re)
            )
        fields = sandwich(fields, PROP, *buffers)
        low_re, low_im = window[position, 0, 1], window[position, 1, 1]
        exits = []
        for mode, (re, im) in enumerate(fields):
            moved[position, 0, mode] = re
            moved[position, 1, mode] = im
            exits.append((re * low_re - im * low_im, re * low_im + im * low_re))
        fields = sandwich(exits, FOUR, *buffers)
        total = jnp.zeros((n, n), F32)
        for mode, (re, im) in enumerate(fields):
            far[position, 0, mode] = re
            far[position, 1, mode] = im
            total = total + (re * re + im * im)
        intensity[position] = total
        return carry

    lax.fori_loop(0, window.shape[0], visit, 0)


def forward(count, offsets, tiles, probe, tables, phase):
    n, modes = probe.shape[-1], probe.shape[1]
    tile = tiles[0].shape[-1]
    fields = jax.ShapeDtypeStruct((count,) + probe.shape, F32)
    return pl.pallas_call(
        forward_kernel,
        out_shape=(
            jax.ShapeDtypeStruct((count, 2, 2, n, n), F32),
            fields,
            fields,
            jax.ShapeDtypeStruct((count, n, n), F32),
        ),
        in_specs=[SMEM] + [ANY] * 6 + [VMEM] * 3,
        out_specs=(VMEM,) * 4,
        scratch_shapes=sandwich_scratch(n, modes)
        + [pltpu.VMEM((2, 2, 3 * tile, 3 * tile), F32), pltpu.SemaphoreType.DMA((9,))],
        compiler_params=pltpu.CompilerParams(vmem_limit_bytes=SCOPED_F << 20),
        cost_estimate=pl.CostEstimate(
            flops=count * modes * 8 * 12 * n**3, bytes_accessed=18 << 20, transcendentals=0
        ),
        name="forward",
    )(offsets, *tiles, probe, tables, phase)


def backward_kernel(
    core, window, moved, far, intensity, measured, probe, tables, phase,
    totals, kept, sent,
    lhs_high, lhs_low, rhs_high, rhs_low, probe_grad, amplitude, sems,
):
    n, modes = probe.shape[-1], probe.shape[1]
    buffers = (tables, lhs_high, lhs_low, rhs_high, rhs_low)
    count = measured.shape[0]
    for at, plane in enumerate(folded([measured[at] for at in range(count)])):
        amplitude[at] = plane

    def visit(position, carry):
        scaling = 1.0 - amplitude[position] / jnp.sqrt(intensity[position] + 1.0)
        fields = [
            (scaling * far[position, 0, mode], scaling * far[position, 1, mode])
            for mode in range(modes)
        ]
        fields = sandwich(fields, FOUR_CONJ, *buffers)
        low_re, low_im = window[position, 0, 1], window[position, 1, 1]
        total_re = total_im = jnp.zeros((n, n), F32)
        behinds = []
        for mode, (re, im) in enumerate(fields):
            moved_re, moved_im = moved[position, 0, mode], moved[position, 1, mode]
            total_re = total_re + (moved_re * re + moved_im * im)
            total_im = total_im + (moved_re * im - moved_im * re)
            behinds.append((low_re * re + low_im * im, low_re * im - low_im * re))
        totals[position, 0, 1] = total_re * phase[0] + total_im * phase[1]
        totals[position, 1, 1] = total_im * phase[0] - total_re * phase[1]
        fields = sandwich(behinds, PROP_CONJ, *buffers)
        top_re, top_im = window[position, 0, 0], window[position, 1, 0]
        total_re = total_im = jnp.zeros((n, n), F32)
        for mode, (re, im) in enumerate(fields):
            probe_re, probe_im = probe[0, mode], probe[1, mode]
            total_re = total_re + (probe_re * re + probe_im * im)
            total_im = total_im + (probe_re * im - probe_im * re)
            term_re = top_re * re + top_im * im
            term_im = top_re * im - top_im * re

            @pl.when(position == 0)
            def _():
                probe_grad[0, mode] = term_re
                probe_grad[1, mode] = term_im

            @pl.when(position != 0)
            def _():
                probe_grad[0, mode] += term_re
                probe_grad[1, mode] += term_im

        totals[position, 0, 0] = total_re
        totals[position, 1, 0] = total_im
        return carry

    lax.fori_loop(0, window.shape[0], visit, 0)

    def unfold(part, carry):
        planes = folded([probe_grad[part, mode] for mode in range(modes)])
        for mode in range(modes):
            probe_grad[part, mode] = planes[mode]
        return carry

    lax.fori_loop(0, 2, unfold, 0)
    copies = [
        pltpu.make_async_copy(probe_grad.at[part], target, sems.at[at])
        for at, (part, target) in enumerate(((core[0], kept), (1 - core[0], sent)))
    ]
    for copy in copies:
        copy.start()
    for copy in copies:
        copy.wait()


def backward(core, state, measured, probe, tables, phase):
    n, modes = probe.shape[-1], probe.shape[1]
    count = measured.shape[0]
    half = jax.ShapeDtypeStruct(probe.shape[1:], F32)
    return pl.pallas_call(
        backward_kernel,
        out_shape=(jax.ShapeDtypeStruct((count, 2, 2, n, n), F32), half, half),
        in_specs=[SMEM] + [VMEM] * 8,
        out_specs=(VMEM, HBM, HBM),
        scratch_shapes=sandwich_scratch(n, modes)
        + [
            pltpu.VMEM(probe.shape, F32),
            pltpu.VMEM(measured.shape, F32),
            pltpu.SemaphoreType.DMA((2,)),
        ],
        compiler_params=pltpu.CompilerParams(vmem_limit_bytes=SCOPED_B << 20),
        cost_estimate=pl.CostEstimate(
            flops=count * modes * 8 * 12 * n**3, bytes_accessed=18 << 20, transcendentals=count * n * n
        ),
        name="backward",
    )(core, *state, measured, probe, tables, phase)


def place_kernel(scalars, totals, grad_left, grad_middle, grad_right, wide, sems):
    n = totals.shape[-1]
    rows, tile = wide.shape[2], wide.shape[3] // 3

    def visit(position, carry):
        row, col = scalars[position, 0], scalars[position, 1]
        at = [(part, layer) for layer in range(2) for part in range(2)]
        planes = folded([totals[position, part, layer] for part, layer in at])
        for (part, layer), plane in zip(at, planes):
            plane = jnp.concatenate([plane, jnp.zeros((rows - n, n), F32)], axis=0)
            plane = pltpu.roll(plane, row, 0)
            plane = jnp.concatenate([plane, jnp.zeros((rows, 3 * tile - n), F32)], axis=1)
            plane = pltpu.roll(plane, col, 1)

            @pl.when(position == 0)
            def _():
                wide[part, layer] = plane

            @pl.when(position != 0)
            def _():
                wide[part, layer] += plane

        return carry

    lax.fori_loop(0, totals.shape[0], visit, 0)
    copies = [
        pltpu.make_async_copy(wide.at[:, :, :, at * tile : (at + 1) * tile], target, sems.at[at])
        for at, target in enumerate((grad_left, grad_middle, grad_right))
    ]
    for copy in copies:
        copy.start()
    for copy in copies:
        copy.wait()


def placed(scalars, totals, rows, tile):
    column = jax.ShapeDtypeStruct((2, 2, rows, tile), F32)
    return pl.pallas_call(
        place_kernel,
        out_shape=(column,) * 3,
        in_specs=[SMEM, VMEM],
        out_specs=(HBM,) * 3,
        scratch_shapes=[pltpu.VMEM((2, 2, rows, 3 * tile), F32), pltpu.SemaphoreType.DMA((3,))],
        compiler_params=pltpu.CompilerParams(vmem_limit_bytes=16 << 20),
        cost_estimate=pl.CostEstimate(flops=2 << 30, bytes_accessed=8 << 20, transcendentals=0),
        name="place",
    )(scalars, totals)


SCOPED_F, SCOPED_B = 20, 20


def around(value, axis, steps):
    count = lax.axis_size(axis)
    return lax.ppermute(value, axis, [(at, (at + steps) % count) for at in range(count)])


def exchanged(value, axis, groups=None):
    return lax.all_to_all(value, axis, 0, 0, tiled=True, axis_index_groups=groups)


def copies(value, count):
    return jnp.broadcast_to(value[None], (count,) + value.shape)


def swapped(value):
    return lax.ppermute(value, "tile", [(at, at ^ 1) for at in range(lax.axis_size("tile"))])


def per_device(object_field, probe_modes, offsets, measured):
    n = probe_modes.shape[-1]
    tile = object_field.shape[2]
    strips, tiles = lax.axis_size("strip"), lax.axis_size("tile")
    both = ("strip", "tile")
    blocks, phase = parity_tables(n)
    phase = jnp.asarray(phase)
    diagonal = [
        (s * tiles + t, (s + 1) % strips * tiles + (t + 1) % tiles)
        for s in range(strips)
        for t in range(tiles)
    ]
    corner = jnp.stack([lax.axis_index("strip"), lax.axis_index("tile")]).astype(jnp.int32) * tile
    wrap = jnp.array([strips * tile, tiles * tile], jnp.int32)
    scalars = lax.ppermute((offsets - corner) % wrap, both, diagonal)
    above = around(object_field, "strip", 1)
    below = around(object_field, "strip", -1)
    left = around(object_field, "tile", 1)
    right = around(object_field, "tile", -1)
    above, below, left, right, scalars, measured = lax.optimization_barrier(
        (above, below, left, right, scalars, measured)
    )
    probe, tables = prepared(probe_modes, jnp.asarray(blocks))
    edges = jnp.concatenate([above, below], axis=2)
    left_edges = around(edges, "tile", 1)
    right_edges = around(edges, "tile", -1)
    measured = lax.ppermute(measured, both, diagonal)
    pieces = (left, left_edges, object_field, edges, right, right_edges)
    state = forward(measured.shape[0], scalars, pieces, probe, tables, phase)
    core = (lax.axis_index("tile") % 2).astype(jnp.int32)
    totals, kept, sent = backward(core.reshape(1), state, measured, probe, tables, phase)

    cores, pairs = 2, 2
    levels = tiles // cores
    groups = [
        [s * tiles + (pairs * group + at) * cores + c for s in range(strips) for at in range(pairs)]
        for c in range(cores)
        for group in range(levels // pairs)
    ]
    received = swapped(sent)
    grad_left, grad_middle, grad_right = placed(scalars, totals, 3 * tile, tile)
    received, grad_left, grad_middle, grad_right = lax.optimization_barrier(
        (received, grad_left, grad_middle, grad_right)
    )
    from_right = around(grad_left, "tile", -1)
    from_left = around(grad_right, "tile", 1)
    shares = exchanged((kept + received).reshape(strips, -1, n), "strip")
    column = grad_middle + from_right + from_left
    upper, lower = column[:, :, :tile], column[:, :, 2 * tile :]
    from_below = around(upper, "strip", -1)
    from_above = around(lower, "strip", 1)
    shares, from_below, from_above = lax.optimization_barrier((shares, from_below, from_above))

    def across(value, distance):
        step = [
            (z * cores + c, (z ^ distance) * cores + c) for z in range(levels) for c in range(cores)
        ]
        return lax.ppermute(value, "tile", step)

    shares = jnp.sum(shares, axis=0).reshape(pairs, -1, n)
    mine = lax.axis_index("tile") // cores % pairs
    share = lax.dynamic_index_in_dim(shares, mine, 0, False) + across(
        lax.dynamic_index_in_dim(shares, 1 - mine, 0, False), 1
    )
    distance = pairs
    while distance < levels:
        share = share + across(share, distance)
        distance *= 2
    object_grad = column[:, :, tile : 2 * tile] + from_below + from_above
    half = exchanged(copies(share, strips * pairs), both, groups)
    other = swapped(half)
    mine = (jnp.arange(cores) == lax.axis_index("tile") % cores).reshape(cores, 1, 1, 1)
    whole = jnp.where(mine, half[None], other[None])
    return (object_grad, whole.reshape(probe_modes.shape))


def solution(mesh):
    in_specs = (
        P(None, None, "strip", "tile"),
        P(),
        P(("strip", "tile"), None),
        P(("strip", "tile"), None, None),
    )
    out_specs = (P(None, None, "strip", "tile"), P())
    return jax.shard_map(
        per_device, mesh=mesh, in_specs=in_specs, out_specs=out_specs, check_vma=False
    )
```

```python
import jax
import jax.numpy as jnp
import ml_dtypes
import numpy as np
from jax import lax
from jax.experimental import pallas as pl
from jax.experimental.pallas import tpu as pltpu
from jax.sharding import PartitionSpec as P

FRESNEL = 0.5
BF, F32 = jnp.bfloat16, jnp.float32
FOUR, FOUR_CONJ, PROP, PROP_CONJ = 0, 1, 2, 3
CHUNK = 1
VMEM = pl.BlockSpec(memory_space=pltpu.VMEM)
SMEM = pl.BlockSpec(memory_space=pltpu.SMEM)
ANY = pl.BlockSpec(memory_space=pl.ANY)
HBM = pl.BlockSpec(memory_space=pltpu.HBM)


def parity_tables(length):
    half = length // 2
    counter = np.arange(length)
    angles = (counter[:, None] * counter[None, :] % length) * (2 * np.pi / length)
    four = np.exp(-1j * angles) / np.sqrt(length)
    mirrored = np.concatenate([counter[:half], counter[:half - 1:-1]])
    quarter = counter - (length - 1) / 2
    shifted = np.exp(-2j * np.pi * quarter[:, None] * quarter[None, :] / length) / np.sqrt(length)
    centred = (counter + half) % length - half
    kern = np.exp(-1j * np.pi * FRESNEL * centred * centred / length)
    prop = (np.conj(four) * kern[None, :]) @ four
    blocks = []
    for matrix in (shifted, prop):
        folded = matrix[mirrored][:, mirrored]
        same, cross = folded[:half, :half], folded[:half, half:]
        even, odd = (same + cross) / 2, (same - cross) / 2
        for part in ("real", "imag"):
            for block in (even, odd):
                value = getattr(block, part)
                high = value.astype(np.float32).astype(ml_dtypes.bfloat16)
                low = (value - high.astype(np.float64)).astype(np.float32)
                blocks += [high, low.astype(ml_dtypes.bfloat16)]
    turn = np.exp(-2j * np.pi * ((length - 1) / 2) * counter / length)[mirrored]
    phase = turn[:, None] * turn[None, :]
    phase = np.stack([phase.real, phase.imag]).astype(np.float32)
    return np.stack(blocks).reshape(2, 2, 2, 2, half, half), phase


def halves(value):
    high = value.astype(BF)
    return high, (value - high.astype(F32)).astype(BF)


def product(a_high, a_low, b_high, b_low):
    total = jnp.dot(a_high, b_high, preferred_element_type=F32)
    total = total + jnp.dot(a_low, b_high, preferred_element_type=F32)
    return total + jnp.dot(a_high, b_low, preferred_element_type=F32)


def anti_diagonal(h):
    row_at = lax.broadcasted_iota(jnp.int32, (h, h), 0)
    col_at = lax.broadcasted_iota(jnp.int32, (h, h), 1)
    return (row_at + col_at == h - 1).astype(F32).astype(BF)


def folded(planes):
    n = planes[0].shape[0]
    h = n // 2
    anti = anti_diagonal(h)
    flipped = jnp.dot(
        jnp.concatenate([jnp.concatenate(halves(plane[:, h:]), axis=1) for plane in planes], axis=0),
        jnp.concatenate([anti, anti], axis=0),
        preferred_element_type=F32,
    )
    planes = [
        jnp.concatenate([plane[:, :h], flipped[at * n : (at + 1) * n]], axis=1)
        for at, plane in enumerate(planes)
    ]
    flipped = jnp.dot(
        jnp.concatenate([anti, anti], axis=1),
        jnp.concatenate([jnp.concatenate(halves(plane[h:]), axis=0) for plane in planes], axis=1),
        preferred_element_type=F32,
    )
    return [
        jnp.concatenate([plane[:h], flipped[:, at * n : (at + 1) * n]], axis=0)
        for at, plane in enumerate(planes)
    ]


def sandwich(fields, which, tables, lhs_high, lhs_low, rhs_high, rhs_low):
    n = tables.shape[-1]
    h = n // 2
    chunks = [range(at, at + CHUNK) for at in range(0, len(fields), CHUNK)]

    def split(chunk):
        for at in chunk:
            for part in range(2):
                first, second = fields[at][part][:, :h], fields[at][part][:, h:]
                for parity, value in enumerate((first + second, first - second)):
                    high, low = halves(value)
                    lhs_high[parity, at * n : (at + 1) * n, part * h : (part + 1) * h] = high
                    lhs_low[parity, at * n : (at + 1) * n, part * h : (part + 1) * h] = low

    def inner(chunk):
        span = slice(chunk[0] * n, (chunk[-1] + 1) * n)
        return [
            product(
                lhs_high[parity, span], lhs_low[parity, span],
                tables[which, parity, 0], tables[which, parity, 1],
            )
            for parity in range(2)
        ]

    def turn(chunk, values):
        for parity, value in enumerate(values):
            for at in chunk:
                base = (at - chunk[0]) * n
                first, second = value[base : base + h], value[base + h : base + n]
                cols = slice(at * n + parity * h, at * n + (parity + 1) * h)
                for turned, mixed in enumerate((first + second, first - second)):
                    high, low = halves(mixed)
                    rhs_high[turned, :h, cols] = high[:, :h]
                    rhs_high[turned, h:, cols] = high[:, h:]
                    rhs_low[turned, :h, cols] = low[:, :h]
                    rhs_low[turned, h:, cols] = low[:, h:]

    def outer(chunk):
        span = slice(chunk[0] * n, (chunk[-1] + 1) * n)
        return [
            product(
                tables[which ^ 1, turned, 0], tables[which ^ 1, turned, 1],
                rhs_high[turned, :, span], rhs_low[turned, :, span],
            )
            for turned in range(2)
        ]

    def joined(chunk, values):
        results = []
        for at in chunk:
            base = (at - chunk[0]) * n
            pair = []
            for part in range(2):
                e = values[0][part * h : (part + 1) * h, base : base + n]
                o = values[1][part * h : (part + 1) * h, base : base + n]
                value = jnp.concatenate([e + o, e - o], axis=0)
                first, second = value[:, :h], value[:, h:]
                pair.append(jnp.concatenate([first + second, first - second], axis=1))
            results.append(pair)
        return results

    results = []
    middle, last = {}, {}
    steps = len(chunks)
    split(chunks[0])
    for at in range(steps):
        middle[at] = inner(chunks[at])
        if at + 1 < steps:
            split(chunks[at + 1])
        if at > 0:
            last[at - 1] = outer(chunks[at - 1])
        turn(chunks[at], middle[at])
        if at > 0:
            results += joined(chunks[at - 1], last[at - 1])
    last[steps - 1] = outer(chunks[steps - 1])
    results += joined(chunks[steps - 1], last[steps - 1])
    return results


def sandwich_scratch(n, modes):
    return [
        pltpu.VMEM((2, modes * n, n), BF),
        pltpu.VMEM((2, modes * n, n), BF),
        pltpu.VMEM((2, n, modes * n), BF),
        pltpu.VMEM((2, n, modes * n), BF),
    ]


def prepare_kernel(probe_in, blocks, probe, tables):
    h = blocks.shape[-1]
    for field in range(2):
        for parity in range(2):
            for part in range(2):
                re, im = blocks[field, 0, parity, part], blocks[field, 1, parity, part]
                for conj in range(2):
                    which = 2 * field + conj
                    upper, lower = (im, -im) if conj == 0 else (-im, im)
                    tables[which, parity, part, :h, :h] = re
                    tables[which, parity, part, h:, h:] = re
                    tables[which, parity, part, :h, h:] = upper
                    tables[which, parity, part, h:, :h] = lower

    def fold(part, carry):
        planes = folded([probe_in[part, mode] for mode in range(probe.shape[1])])
        for mode, plane in enumerate(planes):
            probe[part, mode] = plane
        return carry

    lax.fori_loop(0, 2, fold, 0)


def prepared(probe, blocks):
    n = probe.shape[-1]
    return pl.pallas_call(
        prepare_kernel,
        out_shape=(
            jax.ShapeDtypeStruct(probe.shape, F32),
            jax.ShapeDtypeStruct((4, 2, 2, n, n), BF),
        ),
        in_specs=[VMEM] * 2,
        out_specs=(VMEM,) * 2,
        compiler_params=pltpu.CompilerParams(vmem_limit_bytes=24 << 20),
        cost_estimate=pl.CostEstimate(flops=3 << 30, bytes_accessed=6 << 20, transcendentals=0),
        name="prepare",
    )(probe, blocks)


def forward_kernel(
    left, left_edges, middle, middle_edges, right, right_edges, probe, tables, phase,
    window, moved, far, intensity, offsets,
    lhs_high, lhs_low, rhs_high, rhs_low, wide, numbers, sems,
):
    n, modes = probe.shape[-1], probe.shape[1]
    rows, tile = wide.shape[2], wide.shape[3] // 3
    pieces = []
    for across, (own, edges) in enumerate(
        ((left, left_edges), (middle, middle_edges), (right, right_edges))
    ):
        sources = (edges.at[:, :, :tile], own, edges.at[:, :, tile + 8 :])
        for down, source in enumerate(sources):
            place = wide.at[
                :, :, down * tile : (down + 1) * tile, across * tile : (across + 1) * tile
            ]
            pieces.append(pltpu.make_async_copy(source, place, sems.at[len(pieces)]))
    pieces.append(
        pltpu.make_async_copy(left_edges.at[:, :, tile : tile + 8], numbers, sems.at[len(pieces)])
    )
    for piece in pieces:
        piece.start()
    for piece in pieces:
        piece.wait()
    for position in range(window.shape[0]):
        for axis in range(2):
            offsets[position, axis] = numbers[position, axis, 0, 0].astype(jnp.int32)
    buffers = (tables, lhs_high, lhs_low, rhs_high, rhs_low)

    def visit(position, carry):
        row, col = offsets[position, 0], offsets[position, 1]
        planes = []
        for layer in range(2):
            for part in range(2):
                plane = pltpu.roll(wide[part, layer], 3 * tile - col, 1)[:, :n]
                planes.append(pltpu.roll(plane, rows - row, 0)[:n])
        planes = folded(planes)
        window[position, 0, 0], window[position, 1, 0] = planes[0], planes[1]
        window[position, 0, 1] = planes[2] * phase[0] - planes[3] * phase[1]
        window[position, 1, 1] = planes[2] * phase[1] + planes[3] * phase[0]
        top_re, top_im = window[position, 0, 0], window[position, 1, 0]
        fields = []
        for mode in range(modes):
            probe_re, probe_im = probe[0, mode], probe[1, mode]
            fields.append(
                (probe_re * top_re - probe_im * top_im, probe_re * top_im + probe_im * top_re)
            )
        fields = sandwich(fields, PROP, *buffers)
        low_re, low_im = window[position, 0, 1], window[position, 1, 1]
        exits = []
        for mode, (re, im) in enumerate(fields):
            moved[position, 0, mode] = re
            moved[position, 1, mode] = im
            exits.append((re * low_re - im * low_im, re * low_im + im * low_re))
        fields = sandwich(exits, FOUR, *buffers)
        total = jnp.zeros((n, n), F32)
        for mode, (re, im) in enumerate(fields):
            far[position, 0, mode] = re
            far[position, 1, mode] = im
            total = total + (re * re + im * im)
        intensity[position] = total
        return carry

    lax.fori_loop(0, window.shape[0], visit, 0)


def forward(count, tiles, probe, tables, phase):
    n, modes = probe.shape[-1], probe.shape[1]
    tile = tiles[0].shape[-1]
    fields = jax.ShapeDtypeStruct((count,) + probe.shape, F32)
    return pl.pallas_call(
        forward_kernel,
        out_shape=(
            jax.ShapeDtypeStruct((count, 2, 2, n, n), F32),
            fields,
            fields,
            jax.ShapeDtypeStruct((count, n, n), F32),
            jax.ShapeDtypeStruct((count, 2), jnp.int32),
        ),
        in_specs=[ANY] * 6 + [VMEM] * 3,
        out_specs=(VMEM,) * 4 + (SMEM,),
        scratch_shapes=sandwich_scratch(n, modes)
        + [
            pltpu.VMEM((2, 2, 3 * tile, 3 * tile), F32),
            pltpu.SMEM((2, 2, 8, tile), F32),
            pltpu.SemaphoreType.DMA((10,)),
        ],
        compiler_params=pltpu.CompilerParams(vmem_limit_bytes=SCOPED_F << 20),
        cost_estimate=pl.CostEstimate(
            flops=count * modes * 8 * 12 * n**3, bytes_accessed=18 << 20, transcendentals=0
        ),
        name="forward",
    )(*tiles, probe, tables, phase)


def backward_kernel(
    core, window, moved, far, intensity, measured, probe, tables, phase,
    totals, kept, sent,
    lhs_high, lhs_low, rhs_high, rhs_low, probe_grad, amplitude, sems,
):
    n, modes = probe.shape[-1], probe.shape[1]
    buffers = (tables, lhs_high, lhs_low, rhs_high, rhs_low)
    count = measured.shape[0]
    for at, plane in enumerate(folded([measured[at] for at in range(count)])):
        amplitude[at] = plane

    def visit(position, carry):
        scaling = 1.0 - amplitude[position] / jnp.sqrt(intensity[position] + 1.0)
        fields = [
            (scaling * far[position, 0, mode], scaling * far[position, 1, mode])
            for mode in range(modes)
        ]
        fields = sandwich(fields, FOUR_CONJ, *buffers)
        low_re, low_im = window[position, 0, 1], window[position, 1, 1]
        total_re = total_im = jnp.zeros((n, n), F32)
        behinds = []
        for mode, (re, im) in enumerate(fields):
            moved_re, moved_im = moved[position, 0, mode], moved[position, 1, mode]
            total_re = total_re + (moved_re * re + moved_im * im)
            total_im = total_im + (moved_re * im - moved_im * re)
            behinds.append((low_re * re + low_im * im, low_re * im - low_im * re))
        totals[position, 0, 1] = total_re * phase[0] + total_im * phase[1]
        totals[position, 1, 1] = total_im * phase[0] - total_re * phase[1]
        fields = sandwich(behinds, PROP_CONJ, *buffers)
        top_re, top_im = window[position, 0, 0], window[position, 1, 0]
        total_re = total_im = jnp.zeros((n, n), F32)
        for mode, (re, im) in enumerate(fields):
            probe_re, probe_im = probe[0, mode], probe[1, mode]
            total_re = total_re + (probe_re * re + probe_im * im)
            total_im = total_im + (probe_re * im - probe_im * re)
            term_re = top_re * re + top_im * im
            term_im = top_re * im - top_im * re

            @pl.when(position == 0)
            def _():
                probe_grad[0, mode] = term_re
                probe_grad[1, mode] = term_im

            @pl.when(position != 0)
            def _():
                probe_grad[0, mode] += term_re
                probe_grad[1, mode] += term_im

        totals[position, 0, 0] = total_re
        totals[position, 1, 0] = total_im
        return carry

    lax.fori_loop(0, window.shape[0], visit, 0)

    def unfold(part, carry):
        planes = folded([probe_grad[part, mode] for mode in range(modes)])
        for mode in range(modes):
            probe_grad[part, mode] = planes[mode]
        return carry

    lax.fori_loop(0, 2, unfold, 0)
    copies = [
        pltpu.make_async_copy(probe_grad.at[part], target, sems.at[at])
        for at, (part, target) in enumerate(((core[0], kept), (1 - core[0], sent)))
    ]
    for copy in copies:
        copy.start()
    for copy in copies:
        copy.wait()


def backward(core, state, measured, probe, tables, phase):
    n, modes = probe.shape[-1], probe.shape[1]
    count = measured.shape[0]
    half = jax.ShapeDtypeStruct(probe.shape[1:], F32)
    return pl.pallas_call(
        backward_kernel,
        out_shape=(jax.ShapeDtypeStruct((count, 2, 2, n, n), F32), half, half),
        in_specs=[SMEM] + [VMEM] * 8,
        out_specs=(VMEM, HBM, HBM),
        scratch_shapes=sandwich_scratch(n, modes)
        + [
            pltpu.VMEM(probe.shape, F32),
            pltpu.VMEM(measured.shape, F32),
            pltpu.SemaphoreType.DMA((2,)),
        ],
        compiler_params=pltpu.CompilerParams(vmem_limit_bytes=SCOPED_B << 20),
        cost_estimate=pl.CostEstimate(
            flops=count * modes * 8 * 12 * n**3, bytes_accessed=18 << 20, transcendentals=count * n * n
        ),
        name="backward",
    )(core, *state, measured, probe, tables, phase)


def place_kernel(scalars, totals, grad_left, grad_middle, grad_right, wide, sems):
    n = totals.shape[-1]
    rows, tile = wide.shape[2], wide.shape[3] // 3

    def visit(position, carry):
        row, col = scalars[position, 0], scalars[position, 1]
        at = [(part, layer) for layer in range(2) for part in range(2)]
        planes = folded([totals[position, part, layer] for part, layer in at])
        for (part, layer), plane in zip(at, planes):
            plane = jnp.concatenate([plane, jnp.zeros((rows - n, n), F32)], axis=0)
            plane = pltpu.roll(plane, row, 0)
            plane = jnp.concatenate([plane, jnp.zeros((rows, 3 * tile - n), F32)], axis=1)
            plane = pltpu.roll(plane, col, 1)

            @pl.when(position == 0)
            def _():
                wide[part, layer] = plane

            @pl.when(position != 0)
            def _():
                wide[part, layer] += plane

        return carry

    lax.fori_loop(0, totals.shape[0], visit, 0)
    copies = [
        pltpu.make_async_copy(wide.at[:, :, :, at * tile : (at + 1) * tile], target, sems.at[at])
        for at, target in enumerate((grad_left, grad_middle, grad_right))
    ]
    for copy in copies:
        copy.start()
    for copy in copies:
        copy.wait()


def placed(scalars, totals, rows, tile):
    column = jax.ShapeDtypeStruct((2, 2, rows, tile), F32)
    return pl.pallas_call(
        place_kernel,
        out_shape=(column,) * 3,
        in_specs=[SMEM, VMEM],
        out_specs=(HBM,) * 3,
        scratch_shapes=[pltpu.VMEM((2, 2, rows, 3 * tile), F32), pltpu.SemaphoreType.DMA((3,))],
        compiler_params=pltpu.CompilerParams(vmem_limit_bytes=16 << 20),
        cost_estimate=pl.CostEstimate(flops=2 << 30, bytes_accessed=8 << 20, transcendentals=0),
        name="place",
    )(scalars, totals)


SCOPED_F, SCOPED_B = 20, 20


def around(value, axis, steps):
    count = lax.axis_size(axis)
    return lax.ppermute(value, axis, [(at, (at + steps) % count) for at in range(count)])


def exchanged(value, axis, groups=None):
    return lax.all_to_all(value, axis, 0, 0, tiled=True, axis_index_groups=groups)


def copies(value, count):
    return jnp.broadcast_to(value[None], (count,) + value.shape)


def swapped(value):
    return lax.ppermute(value, "tile", [(at, at ^ 1) for at in range(lax.axis_size("tile"))])


def per_device(object_field, probe_modes, offsets, measured):
    n = probe_modes.shape[-1]
    tile = object_field.shape[2]
    strips, tiles = lax.axis_size("strip"), lax.axis_size("tile")
    both = ("strip", "tile")
    blocks, phase = parity_tables(n)
    phase = jnp.asarray(phase)
    diagonal = [
        (s * tiles + t, (s + 1) % strips * tiles + (t + 1) % tiles)
        for s in range(strips)
        for t in range(tiles)
    ]
    corner = jnp.stack([lax.axis_index("strip"), lax.axis_index("tile")]).astype(jnp.int32) * tile
    wrap = jnp.array([strips * tile, tiles * tile], jnp.int32)
    local = ((offsets - corner) % wrap).astype(F32)[:, :, None, None]
    sent_down = jnp.concatenate(
        [object_field, jnp.broadcast_to(local, local.shape[:2] + (8, tile))], axis=2
    )
    above = around(sent_down, "strip", 1)
    below = around(object_field, "strip", -1)
    left = around(object_field, "tile", 1)
    right = around(object_field, "tile", -1)
    above, below, left, right, measured = lax.optimization_barrier(
        (above, below, left, right, measured)
    )
    probe, tables = prepared(probe_modes, jnp.asarray(blocks))
    edges = jnp.concatenate([above, below], axis=2)
    left_edges = around(edges, "tile", 1)
    right_edges = around(edges, "tile", -1)
    measured = lax.ppermute(measured, both, diagonal)
    pieces = (left, left_edges, object_field, edges, right, right_edges)
    *state, scalars = forward(measured.shape[0], pieces, probe, tables, phase)
    core = (lax.axis_index("tile") % 2).astype(jnp.int32)
    totals, kept, sent = backward(core.reshape(1), state, measured, probe, tables, phase)

    cores, pairs = 2, 2
    levels = tiles // cores
    groups = [
        [s * tiles + (pairs * group + at) * cores + c for s in range(strips) for at in range(pairs)]
        for c in range(cores)
        for group in range(levels // pairs)
    ]
    part = (kept + swapped(sent)).reshape(strips, -1, n)
    part, totals = lax.optimization_barrier((part, totals))
    shares = exchanged(part, "strip")
    grad_left, grad_middle, grad_right = placed(scalars, totals, 3 * tile, tile)
    from_right = around(grad_left, "tile", -1)
    from_left = around(grad_right, "tile", 1)
    shares, from_right, from_left = lax.optimization_barrier((shares, from_right, from_left))
    column = grad_middle + from_right + from_left
    upper, lower = column[:, :, :tile], column[:, :, 2 * tile :]
    from_below = around(upper, "strip", -1)
    from_above = around(lower, "strip", 1)

    def across(value, distance):
        step = [
            (z * cores + c, (z ^ distance) * cores + c) for z in range(levels) for c in range(cores)
        ]
        return lax.ppermute(value, "tile", step)

    shares = jnp.sum(shares, axis=0).reshape(pairs, -1, n)
    mine = lax.axis_index("tile") // cores % pairs
    share = lax.dynamic_index_in_dim(shares, mine, 0, False) + across(
        lax.dynamic_index_in_dim(shares, 1 - mine, 0, False), 1
    )
    distance = pairs
    while distance < levels:
        share = share + across(share, distance)
        distance *= 2
    share, from_below, from_above = lax.optimization_barrier((share, from_below, from_above))
    object_grad = column[:, :, tile : 2 * tile] + from_below + from_above
    half = exchanged(copies(share, strips * pairs), both, groups)
    other = swapped(half)
    mine = (jnp.arange(cores) == lax.axis_index("tile") % cores).reshape(cores, 1, 1, 1)
    whole = jnp.where(mine, half[None], other[None])
    return (object_grad, whole.reshape(probe_modes.shape))


def solution(mesh):
    in_specs = (
        P(None, None, "strip", "tile"),
        P(),
        P(("strip", "tile"), None),
        P(("strip", "tile"), None, None),
    )
    out_specs = (P(None, None, "strip", "tile"), P())
    return jax.shard_map(
        per_device, mesh=mesh, in_specs=in_specs, out_specs=out_specs, check_vma=False
    )
```

```python
import jax
import jax.numpy as jnp
import ml_dtypes
import numpy as np
from jax import lax
from jax.experimental import pallas as pl
from jax.experimental.pallas import tpu as pltpu
from jax.sharding import PartitionSpec as P

FRESNEL = 0.5
BF, F32 = jnp.bfloat16, jnp.float32
FOUR, FOUR_CONJ, PROP, PROP_CONJ = 0, 1, 2, 3
CHUNK = 1
VMEM = pl.BlockSpec(memory_space=pltpu.VMEM)
SMEM = pl.BlockSpec(memory_space=pltpu.SMEM)
ANY = pl.BlockSpec(memory_space=pl.ANY)
HBM = pl.BlockSpec(memory_space=pltpu.HBM)


def parity_tables(length):
    half = length // 2
    counter = np.arange(length)
    angles = (counter[:, None] * counter[None, :] % length) * (2 * np.pi / length)
    four = np.exp(-1j * angles) / np.sqrt(length)
    mirrored = np.concatenate([counter[:half], counter[:half - 1:-1]])
    quarter = counter - (length - 1) / 2
    shifted = np.exp(-2j * np.pi * quarter[:, None] * quarter[None, :] / length) / np.sqrt(length)
    centred = (counter + half) % length - half
    kern = np.exp(-1j * np.pi * FRESNEL * centred * centred / length)
    prop = (np.conj(four) * kern[None, :]) @ four
    blocks = []
    for matrix in (shifted, prop):
        folded = matrix[mirrored][:, mirrored]
        same, cross = folded[:half, :half], folded[:half, half:]
        even, odd = (same + cross) / 2, (same - cross) / 2
        for part in ("real", "imag"):
            for block in (even, odd):
                value = getattr(block, part)
                high = value.astype(np.float32).astype(ml_dtypes.bfloat16)
                low = (value - high.astype(np.float64)).astype(np.float32)
                blocks += [high, low.astype(ml_dtypes.bfloat16)]
    turn = np.exp(-2j * np.pi * ((length - 1) / 2) * counter / length)[mirrored]
    phase = turn[:, None] * turn[None, :]
    phase = np.stack([phase.real, phase.imag]).astype(np.float32)
    return np.stack(blocks).reshape(2, 2, 2, 2, half, half), phase


def halves(value):
    high = value.astype(BF)
    return high, (value - high.astype(F32)).astype(BF)


def product(a_high, a_low, b_high, b_low):
    total = jnp.dot(a_high, b_high, preferred_element_type=F32)
    total = total + jnp.dot(a_low, b_high, preferred_element_type=F32)
    return total + jnp.dot(a_high, b_low, preferred_element_type=F32)


def anti_diagonal(h):
    row_at = lax.broadcasted_iota(jnp.int32, (h, h), 0)
    col_at = lax.broadcasted_iota(jnp.int32, (h, h), 1)
    return (row_at + col_at == h - 1).astype(F32).astype(BF)


def folded(planes):
    n = planes[0].shape[0]
    h = n // 2
    anti = anti_diagonal(h)
    flipped = jnp.dot(
        jnp.concatenate([jnp.concatenate(halves(plane[:, h:]), axis=1) for plane in planes], axis=0),
        jnp.concatenate([anti, anti], axis=0),
        preferred_element_type=F32,
    )
    planes = [
        jnp.concatenate([plane[:, :h], flipped[at * n : (at + 1) * n]], axis=1)
        for at, plane in enumerate(planes)
    ]
    flipped = jnp.dot(
        jnp.concatenate([anti, anti], axis=1),
        jnp.concatenate([jnp.concatenate(halves(plane[h:]), axis=0) for plane in planes], axis=1),
        preferred_element_type=F32,
    )
    return [
        jnp.concatenate([plane[:h], flipped[:, at * n : (at + 1) * n]], axis=0)
        for at, plane in enumerate(planes)
    ]


def sandwich(fields, which, tables, lhs_high, lhs_low, rhs_high, rhs_low):
    n = tables.shape[-1]
    h = n // 2
    chunks = [range(at, at + CHUNK) for at in range(0, len(fields), CHUNK)]

    def split(chunk):
        for at in chunk:
            for part in range(2):
                first, second = fields[at][part][:, :h], fields[at][part][:, h:]
                for parity, value in enumerate((first + second, first - second)):
                    high, low = halves(value)
                    lhs_high[parity, at * n : (at + 1) * n, part * h : (part + 1) * h] = high
                    lhs_low[parity, at * n : (at + 1) * n, part * h : (part + 1) * h] = low

    def inner(chunk):
        span = slice(chunk[0] * n, (chunk[-1] + 1) * n)
        return [
            product(
                lhs_high[parity, span], lhs_low[parity, span],
                tables[which, parity, 0], tables[which, parity, 1],
            )
            for parity in range(2)
        ]

    def turn(chunk, values):
        for parity, value in enumerate(values):
            for at in chunk:
                base = (at - chunk[0]) * n
                first, second = value[base : base + h], value[base + h : base + n]
                cols = slice(at * n + parity * h, at * n + (parity + 1) * h)
                for turned, mixed in enumerate((first + second, first - second)):
                    high, low = halves(mixed)
                    rhs_high[turned, :h, cols] = high[:, :h]
                    rhs_high[turned, h:, cols] = high[:, h:]
                    rhs_low[turned, :h, cols] = low[:, :h]
                    rhs_low[turned, h:, cols] = low[:, h:]

    def outer(chunk):
        span = slice(chunk[0] * n, (chunk[-1] + 1) * n)
        return [
            product(
                tables[which ^ 1, turned, 0], tables[which ^ 1, turned, 1],
                rhs_high[turned, :, span], rhs_low[turned, :, span],
            )
            for turned in range(2)
        ]

    def joined(chunk, values):
        results = []
        for at in chunk:
            base = (at - chunk[0]) * n
            pair = []
            for part in range(2):
                e = values[0][part * h : (part + 1) * h, base : base + n]
                o = values[1][part * h : (part + 1) * h, base : base + n]
                value = jnp.concatenate([e + o, e - o], axis=0)
                first, second = value[:, :h], value[:, h:]
                pair.append(jnp.concatenate([first + second, first - second], axis=1))
            results.append(pair)
        return results

    results = []
    middle, last = {}, {}
    steps = len(chunks)
    split(chunks[0])
    for at in range(steps):
        middle[at] = inner(chunks[at])
        if at + 1 < steps:
            split(chunks[at + 1])
        if at > 0:
            last[at - 1] = outer(chunks[at - 1])
        turn(chunks[at], middle[at])
        if at > 0:
            results += joined(chunks[at - 1], last[at - 1])
    last[steps - 1] = outer(chunks[steps - 1])
    results += joined(chunks[steps - 1], last[steps - 1])
    return results


def sandwich_scratch(n, modes):
    return [
        pltpu.VMEM((2, modes * n, n), BF),
        pltpu.VMEM((2, modes * n, n), BF),
        pltpu.VMEM((2, n, modes * n), BF),
        pltpu.VMEM((2, n, modes * n), BF),
    ]


def label_kernel(offsets, corner, tile_in, out, sem):
    tile = tile_in.shape[-1]
    copy = pltpu.make_async_copy(tile_in, out.at[:, :, :tile], sem)
    copy.start()
    for position in range(offsets.shape[0]):
        for axis in range(2):
            number = (offsets[position, axis] - corner[axis]).astype(F32)
            out[position, axis, tile:] = jnp.full((8, tile), number, F32)
    copy.wait()


def labelled(offsets, corner, field):
    tile = field.shape[-1]
    return pl.pallas_call(
        label_kernel,
        out_shape=jax.ShapeDtypeStruct(field.shape[:2] + (tile + 8, tile), F32),
        in_specs=[SMEM, SMEM, ANY],
        out_specs=VMEM,
        scratch_shapes=[pltpu.SemaphoreType.DMA],
        compiler_params=pltpu.CompilerParams(vmem_limit_bytes=4 << 20),
        cost_estimate=pl.CostEstimate(flops=0, bytes_accessed=1 << 19, transcendentals=0),
        name="label",
    )(offsets, corner, field)


def prepare_kernel(probe_in, blocks, probe, tables):
    h = blocks.shape[-1]
    for field in range(2):
        for parity in range(2):
            for part in range(2):
                re, im = blocks[field, 0, parity, part], blocks[field, 1, parity, part]
                for conj in range(2):
                    which = 2 * field + conj
                    upper, lower = (im, -im) if conj == 0 else (-im, im)
                    tables[which, parity, part, :h, :h] = re
                    tables[which, parity, part, h:, h:] = re
                    tables[which, parity, part, :h, h:] = upper
                    tables[which, parity, part, h:, :h] = lower

    def fold(part, carry):
        planes = folded([probe_in[part, mode] for mode in range(probe.shape[1])])
        for mode, plane in enumerate(planes):
            probe[part, mode] = plane
        return carry

    lax.fori_loop(0, 2, fold, 0)


def prepared(probe, blocks):
    n = probe.shape[-1]
    return pl.pallas_call(
        prepare_kernel,
        out_shape=(
            jax.ShapeDtypeStruct(probe.shape, F32),
            jax.ShapeDtypeStruct((4, 2, 2, n, n), BF),
        ),
        in_specs=[VMEM] * 2,
        out_specs=(VMEM,) * 2,
        compiler_params=pltpu.CompilerParams(vmem_limit_bytes=24 << 20),
        cost_estimate=pl.CostEstimate(flops=3 << 30, bytes_accessed=6 << 20, transcendentals=0),
        name="prepare",
    )(probe, blocks)


def forward_kernel(
    left, left_edges, middle, middle_edges, right, right_edges, probe, tables, phase,
    window, moved, far, intensity, offsets,
    lhs_high, lhs_low, rhs_high, rhs_low, wide, numbers, sems,
):
    n, modes = probe.shape[-1], probe.shape[1]
    rows, tile = wide.shape[2], wide.shape[3] // 3
    pieces = []
    for across, (own, edges) in enumerate(
        ((left, left_edges), (middle, middle_edges), (right, right_edges))
    ):
        sources = (edges.at[:, :, :tile], own, edges.at[:, :, tile + 8 :])
        for down, source in enumerate(sources):
            place = wide.at[
                :, :, down * tile : (down + 1) * tile, across * tile : (across + 1) * tile
            ]
            pieces.append(pltpu.make_async_copy(source, place, sems.at[len(pieces)]))
    pieces.append(
        pltpu.make_async_copy(left_edges.at[:, :, tile : tile + 8], numbers, sems.at[len(pieces)])
    )
    for piece in pieces:
        piece.start()
    for piece in pieces:
        piece.wait()
    for position in range(window.shape[0]):
        for axis in range(2):
            offsets[position, axis] = numbers[position, axis, 0, 0].astype(jnp.int32)
    buffers = (tables, lhs_high, lhs_low, rhs_high, rhs_low)

    def visit(position, carry):
        row, col = offsets[position, 0], offsets[position, 1]
        planes = []
        for layer in range(2):
            for part in range(2):
                plane = pltpu.roll(wide[part, layer], 3 * tile - col, 1)[:, :n]
                planes.append(pltpu.roll(plane, rows - row, 0)[:n])
        planes = folded(planes)
        window[position, 0, 0], window[position, 1, 0] = planes[0], planes[1]
        window[position, 0, 1] = planes[2] * phase[0] - planes[3] * phase[1]
        window[position, 1, 1] = planes[2] * phase[1] + planes[3] * phase[0]
        top_re, top_im = window[position, 0, 0], window[position, 1, 0]
        fields = []
        for mode in range(modes):
            probe_re, probe_im = probe[0, mode], probe[1, mode]
            fields.append(
                (probe_re * top_re - probe_im * top_im, probe_re * top_im + probe_im * top_re)
            )
        fields = sandwich(fields, PROP, *buffers)
        low_re, low_im = window[position, 0, 1], window[position, 1, 1]
        exits = []
        for mode, (re, im) in enumerate(fields):
            moved[position, 0, mode] = re
            moved[position, 1, mode] = im
            exits.append((re * low_re - im * low_im, re * low_im + im * low_re))
        fields = sandwich(exits, FOUR, *buffers)
        total = jnp.zeros((n, n), F32)
        for mode, (re, im) in enumerate(fields):
            far[position, 0, mode] = re
            far[position, 1, mode] = im
            total = total + (re * re + im * im)
        intensity[position] = total
        return carry

    lax.fori_loop(0, window.shape[0], visit, 0)


def forward(count, tiles, probe, tables, phase):
    n, modes = probe.shape[-1], probe.shape[1]
    tile = tiles[0].shape[-1]
    fields = jax.ShapeDtypeStruct((count,) + probe.shape, F32)
    return pl.pallas_call(
        forward_kernel,
        out_shape=(
            jax.ShapeDtypeStruct((count, 2, 2, n, n), F32),
            fields,
            fields,
            jax.ShapeDtypeStruct((count, n, n), F32),
            jax.ShapeDtypeStruct((count, 2), jnp.int32),
        ),
        in_specs=[ANY] * 6 + [VMEM] * 3,
        out_specs=(VMEM,) * 4 + (SMEM,),
        scratch_shapes=sandwich_scratch(n, modes)
        + [
            pltpu.VMEM((2, 2, 3 * tile, 3 * tile), F32),
            pltpu.SMEM((2, 2, 8, tile), F32),
            pltpu.SemaphoreType.DMA((10,)),
        ],
        compiler_params=pltpu.CompilerParams(vmem_limit_bytes=SCOPED_F << 20),
        cost_estimate=pl.CostEstimate(
            flops=count * modes * 8 * 12 * n**3, bytes_accessed=18 << 20, transcendentals=0
        ),
        name="forward",
    )(*tiles, probe, tables, phase)


def backward_kernel(
    core, window, moved, far, intensity, measured, probe, tables, phase,
    totals, kept, sent,
    lhs_high, lhs_low, rhs_high, rhs_low, probe_grad, amplitude, sems,
):
    n, modes = probe.shape[-1], probe.shape[1]
    buffers = (tables, lhs_high, lhs_low, rhs_high, rhs_low)
    count = measured.shape[0]
    for at, plane in enumerate(folded([measured[at] for at in range(count)])):
        amplitude[at] = plane

    def visit(position, carry):
        scaling = 1.0 - amplitude[position] / jnp.sqrt(intensity[position] + 1.0)
        fields = [
            (scaling * far[position, 0, mode], scaling * far[position, 1, mode])
            for mode in range(modes)
        ]
        fields = sandwich(fields, FOUR_CONJ, *buffers)
        low_re, low_im = window[position, 0, 1], window[position, 1, 1]
        total_re = total_im = jnp.zeros((n, n), F32)
        behinds = []
        for mode, (re, im) in enumerate(fields):
            moved_re, moved_im = moved[position, 0, mode], moved[position, 1, mode]
            total_re = total_re + (moved_re * re + moved_im * im)
            total_im = total_im + (moved_re * im - moved_im * re)
            behinds.append((low_re * re + low_im * im, low_re * im - low_im * re))
        totals[position, 0, 1] = total_re * phase[0] + total_im * phase[1]
        totals[position, 1, 1] = total_im * phase[0] - total_re * phase[1]
        fields = sandwich(behinds, PROP_CONJ, *buffers)
        top_re, top_im = window[position, 0, 0], window[position, 1, 0]
        total_re = total_im = jnp.zeros((n, n), F32)
        for mode, (re, im) in enumerate(fields):
            probe_re, probe_im = probe[0, mode], probe[1, mode]
            total_re = total_re + (probe_re * re + probe_im * im)
            total_im = total_im + (probe_re * im - probe_im * re)
            term_re = top_re * re + top_im * im
            term_im = top_re * im - top_im * re

            @pl.when(position == 0)
            def _():
                probe_grad[0, mode] = term_re
                probe_grad[1, mode] = term_im

            @pl.when(position != 0)
            def _():
                probe_grad[0, mode] += term_re
                probe_grad[1, mode] += term_im

        totals[position, 0, 0] = total_re
        totals[position, 1, 0] = total_im
        return carry

    lax.fori_loop(0, window.shape[0], visit, 0)

    def unfold(part, carry):
        planes = folded([probe_grad[part, mode] for mode in range(modes)])
        for mode in range(modes):
            probe_grad[part, mode] = planes[mode]
        return carry

    lax.fori_loop(0, 2, unfold, 0)
    copies = [
        pltpu.make_async_copy(probe_grad.at[part], target, sems.at[at])
        for at, (part, target) in enumerate(((core[0], kept), (1 - core[0], sent)))
    ]
    for copy in copies:
        copy.start()
    for copy in copies:
        copy.wait()


def backward(core, state, measured, probe, tables, phase):
    n, modes = probe.shape[-1], probe.shape[1]
    count = measured.shape[0]
    half = jax.ShapeDtypeStruct(probe.shape[1:], F32)
    return pl.pallas_call(
        backward_kernel,
        out_shape=(jax.ShapeDtypeStruct((count, 2, 2, n, n), F32), half, half),
        in_specs=[SMEM] + [VMEM] * 8,
        out_specs=(VMEM, HBM, HBM),
        scratch_shapes=sandwich_scratch(n, modes)
        + [
            pltpu.VMEM(probe.shape, F32),
            pltpu.VMEM(measured.shape, F32),
            pltpu.SemaphoreType.DMA((2,)),
        ],
        compiler_params=pltpu.CompilerParams(vmem_limit_bytes=SCOPED_B << 20),
        cost_estimate=pl.CostEstimate(
            flops=count * modes * 8 * 12 * n**3, bytes_accessed=18 << 20, transcendentals=count * n * n
        ),
        name="backward",
    )(core, *state, measured, probe, tables, phase)


def place_kernel(scalars, totals, grad_left, grad_middle, grad_right, wide, sems):
    n = totals.shape[-1]
    rows, tile = wide.shape[2], wide.shape[3] // 3

    def visit(position, carry):
        row, col = scalars[position, 0], scalars[position, 1]
        at = [(part, layer) for layer in range(2) for part in range(2)]
        planes = folded([totals[position, part, layer] for part, layer in at])
        for (part, layer), plane in zip(at, planes):
            plane = jnp.concatenate([plane, jnp.zeros((rows - n, n), F32)], axis=0)
            plane = pltpu.roll(plane, row, 0)
            plane = jnp.concatenate([plane, jnp.zeros((rows, 3 * tile - n), F32)], axis=1)
            plane = pltpu.roll(plane, col, 1)

            @pl.when(position == 0)
            def _():
                wide[part, layer] = plane

            @pl.when(position != 0)
            def _():
                wide[part, layer] += plane

        return carry

    lax.fori_loop(0, totals.shape[0], visit, 0)
    copies = [
        pltpu.make_async_copy(wide.at[:, :, :, at * tile : (at + 1) * tile], target, sems.at[at])
        for at, target in enumerate((grad_left, grad_middle, grad_right))
    ]
    for copy in copies:
        copy.start()
    for copy in copies:
        copy.wait()


def placed(scalars, totals, rows, tile):
    column = jax.ShapeDtypeStruct((2, 2, rows, tile), F32)
    return pl.pallas_call(
        place_kernel,
        out_shape=(column,) * 3,
        in_specs=[SMEM, VMEM],
        out_specs=(HBM,) * 3,
        scratch_shapes=[pltpu.VMEM((2, 2, rows, 3 * tile), F32), pltpu.SemaphoreType.DMA((3,))],
        compiler_params=pltpu.CompilerParams(vmem_limit_bytes=16 << 20),
        cost_estimate=pl.CostEstimate(flops=2 << 30, bytes_accessed=8 << 20, transcendentals=0),
        name="place",
    )(scalars, totals)


SCOPED_F, SCOPED_B = 20, 20


def around(value, axis, steps):
    count = lax.axis_size(axis)
    return lax.ppermute(value, axis, [(at, (at + steps) % count) for at in range(count)])


def exchanged(value, axis, groups=None):
    return lax.all_to_all(value, axis, 0, 0, tiled=True, axis_index_groups=groups)


def copies(value, count):
    return jnp.broadcast_to(value[None], (count,) + value.shape)


def swapped(value):
    return lax.ppermute(value, "tile", [(at, at ^ 1) for at in range(lax.axis_size("tile"))])


def per_device(object_field, probe_modes, offsets, measured):
    n = probe_modes.shape[-1]
    tile = object_field.shape[2]
    strips, tiles = lax.axis_size("strip"), lax.axis_size("tile")
    both = ("strip", "tile")
    blocks, phase = parity_tables(n)
    phase = jnp.asarray(phase)
    diagonal = [
        (s * tiles + t, (s + 1) % strips * tiles + (t + 1) % tiles)
        for s in range(strips)
        for t in range(tiles)
    ]
    corner = jnp.stack([lax.axis_index("strip"), lax.axis_index("tile")]).astype(jnp.int32) * tile
    sent_down = labelled(offsets, corner, object_field)
    above = around(sent_down, "strip", 1)
    below = around(object_field, "strip", -1)
    left = around(object_field, "tile", 1)
    right = around(object_field, "tile", -1)
    above, below, left, right, measured = lax.optimization_barrier(
        (above, below, left, right, measured)
    )
    probe, tables = prepared(probe_modes, jnp.asarray(blocks))
    edges = jnp.concatenate([above, below], axis=2)
    left_edges = around(edges, "tile", 1)
    right_edges = around(edges, "tile", -1)
    measured = lax.ppermute(measured, both, diagonal)
    pieces = (left, left_edges, object_field, edges, right, right_edges)
    *state, scalars = forward(measured.shape[0], pieces, probe, tables, phase)
    core = (lax.axis_index("tile") % 2).astype(jnp.int32)
    totals, kept, sent = backward(core.reshape(1), state, measured, probe, tables, phase)

    cores, pairs = 2, 2
    levels = tiles // cores
    groups = [
        [s * tiles + (pairs * group + at) * cores + c for s in range(strips) for at in range(pairs)]
        for c in range(cores)
        for group in range(levels // pairs)
    ]
    received = swapped(sent)
    grad_left, grad_middle, grad_right = placed(scalars, totals, 3 * tile, tile)
    received, grad_left, grad_middle, grad_right = lax.optimization_barrier(
        (received, grad_left, grad_middle, grad_right)
    )
    from_right = around(grad_left, "tile", -1)
    from_left = around(grad_right, "tile", 1)
    shares = exchanged((kept + received).reshape(strips, -1, n), "strip")
    column = grad_middle + from_right + from_left
    upper, lower = column[:, :, :tile], column[:, :, 2 * tile :]
    from_below = around(upper, "strip", -1)
    from_above = around(lower, "strip", 1)
    shares, column, upper, lower = lax.optimization_barrier((shares, column, upper, lower))

    def across(value, distance):
        step = [
            (z * cores + c, (z ^ distance) * cores + c) for z in range(levels) for c in range(cores)
        ]
        return lax.ppermute(value, "tile", step)

    shares = jnp.sum(shares, axis=0).reshape(pairs, -1, n)
    mine = lax.axis_index("tile") // cores % pairs
    share = lax.dynamic_index_in_dim(shares, mine, 0, False) + across(
        lax.dynamic_index_in_dim(shares, 1 - mine, 0, False), 1
    )
    distance = pairs
    share, from_below, from_above = lax.optimization_barrier((share, from_below, from_above))
    while distance < levels:
        share = share + across(share, distance)
        distance *= 2
    object_grad = column[:, :, tile : 2 * tile] + from_below + from_above
    half = exchanged(copies(share, strips * pairs), both, groups)
    other = swapped(half)
    mine = (jnp.arange(cores) == lax.axis_index("tile") % cores).reshape(cores, 1, 1, 1)
    whole = jnp.where(mine, half[None], other[None])
    return (object_grad, whole.reshape(probe_modes.shape))


def solution(mesh):
    in_specs = (
        P(None, None, "strip", "tile"),
        P(),
        P(("strip", "tile"), None),
        P(("strip", "tile"), None, None),
    )
    out_specs = (P(None, None, "strip", "tile"), P())
    return jax.shard_map(
        per_device, mesh=mesh, in_specs=in_specs, out_specs=out_specs, check_vma=False
    )
```

```python
import jax
import jax.numpy as jnp
import ml_dtypes
import numpy as np
from jax import lax
from jax.experimental import pallas as pl
from jax.experimental.pallas import tpu as pltpu
from jax.sharding import PartitionSpec as P

FRESNEL = 0.5
BF, F32 = jnp.bfloat16, jnp.float32
FOUR, FOUR_CONJ, PROP, PROP_CONJ = 0, 1, 2, 3
STAGGER = 1
VMEM = pl.BlockSpec(memory_space=pltpu.VMEM)
SMEM = pl.BlockSpec(memory_space=pltpu.SMEM)
ANY = pl.BlockSpec(memory_space=pl.ANY)
HBM = pl.BlockSpec(memory_space=pltpu.HBM)


def parity_tables(length):
    half = length // 2
    counter = np.arange(length)
    angles = (counter[:, None] * counter[None, :] % length) * (2 * np.pi / length)
    four = np.exp(-1j * angles) / np.sqrt(length)
    mirrored = np.concatenate([counter[:half], counter[:half - 1:-1]])
    quarter = counter - (length - 1) / 2
    shifted = np.exp(-2j * np.pi * quarter[:, None] * quarter[None, :] / length) / np.sqrt(length)
    centred = (counter + half) % length - half
    kern = np.exp(-1j * np.pi * FRESNEL * centred * centred / length)
    prop = (np.conj(four) * kern[None, :]) @ four
    blocks = []
    for matrix in (shifted, prop):
        folded = matrix[mirrored][:, mirrored]
        same, cross = folded[:half, :half], folded[:half, half:]
        even, odd = (same + cross) / 2, (same - cross) / 2
        for part in ("real", "imag"):
            for block in (even, odd):
                value = getattr(block, part)
                high = value.astype(np.float32).astype(ml_dtypes.bfloat16)
                low = (value - high.astype(np.float64)).astype(np.float32)
                blocks += [high, low.astype(ml_dtypes.bfloat16)]
    turn = np.exp(-2j * np.pi * ((length - 1) / 2) * counter / length)[mirrored]
    phase = turn[:, None] * turn[None, :]
    phase = np.stack([phase.real, phase.imag]).astype(np.float32)
    return np.stack(blocks).reshape(2, 2, 2, 2, half, half), phase


def halves(value):
    high = value.astype(BF)
    return high, (value - high.astype(F32)).astype(BF)


def product(a_high, a_low, b_high, b_low):
    total = jnp.dot(a_high, b_high, preferred_element_type=F32)
    total = total + jnp.dot(a_low, b_high, preferred_element_type=F32)
    return total + jnp.dot(a_high, b_low, preferred_element_type=F32)


def anti_diagonal(h):
    row_at = lax.broadcasted_iota(jnp.int32, (h, h), 0)
    col_at = lax.broadcasted_iota(jnp.int32, (h, h), 1)
    return (row_at + col_at == h - 1).astype(F32).astype(BF)


def folded(planes):
    n = planes[0].shape[0]
    h = n // 2
    anti = anti_diagonal(h)
    flipped = jnp.dot(
        jnp.concatenate([jnp.concatenate(halves(plane[:, h:]), axis=1) for plane in planes], axis=0),
        jnp.concatenate([anti, anti], axis=0),
        preferred_element_type=F32,
    )
    planes = [
        jnp.concatenate([plane[:, :h], flipped[at * n : (at + 1) * n]], axis=1)
        for at, plane in enumerate(planes)
    ]
    flipped = jnp.dot(
        jnp.concatenate([anti, anti], axis=1),
        jnp.concatenate([jnp.concatenate(halves(plane[h:]), axis=0) for plane in planes], axis=1),
        preferred_element_type=F32,
    )
    return [
        jnp.concatenate([plane[:h], flipped[:, at * n : (at + 1) * n]], axis=0)
        for at, plane in enumerate(planes)
    ]


def sandwich(field, which, at, tables, lhs_high, lhs_low, rhs_high, rhs_low):
    n = tables.shape[-1]
    h = n // 2
    rows = slice(at * n, (at + 1) * n)
    for part in range(2):
        first, second = field[part][:, :h], field[part][:, h:]
        for parity, value in enumerate((first + second, first - second)):
            high, low = halves(value)
            lhs_high[parity, rows, part * h : (part + 1) * h] = high
            lhs_low[parity, rows, part * h : (part + 1) * h] = low
    yield
    inner = [
        product(
            lhs_high[parity, rows], lhs_low[parity, rows],
            tables[which, parity, 0], tables[which, parity, 1],
        )
        for parity in range(2)
    ]
    yield
    for parity, value in enumerate(inner):
        first, second = value[:h], value[h:]
        cols = slice(at * n + parity * h, at * n + (parity + 1) * h)
        for turned, mixed in enumerate((first + second, first - second)):
            high, low = halves(mixed)
            rhs_high[turned, :h, cols] = high[:, :h]
            rhs_high[turned, h:, cols] = high[:, h:]
            rhs_low[turned, :h, cols] = low[:, :h]
            rhs_low[turned, h:, cols] = low[:, h:]
    yield
    outer = [
        product(
            tables[which ^ 1, turned, 0], tables[which ^ 1, turned, 1],
            rhs_high[turned, :, rows], rhs_low[turned, :, rows],
        )
        for turned in range(2)
    ]
    yield
    pair = []
    for part in range(2):
        e = outer[0][part * h : (part + 1) * h]
        o = outer[1][part * h : (part + 1) * h]
        value = jnp.concatenate([e + o, e - o], axis=0)
        first, second = value[:, :h], value[:, h:]
        pair.append(jnp.concatenate([first + second, first - second], axis=1))
    return pair


def staggered(chains):
    results = [None] * len(chains)
    running = set(range(len(chains)))
    step = 0
    while running:
        for at in sorted(running):
            if step >= at * STAGGER:
                try:
                    next(chains[at])
                except StopIteration as end:
                    results[at] = end.value
                    running.discard(at)
        step += 1
    return results


def sandwich_scratch(n, modes):
    return [
        pltpu.VMEM((2, modes * n, n), BF),
        pltpu.VMEM((2, modes * n, n), BF),
        pltpu.VMEM((2, n, modes * n), BF),
        pltpu.VMEM((2, n, modes * n), BF),
    ]


def prepare_kernel(probe_in, measured_in, blocks, probe, measured, tables):
    h = blocks.shape[-1]
    for field in range(2):
        for parity in range(2):
            for part in range(2):
                re, im = blocks[field, 0, parity, part], blocks[field, 1, parity, part]
                for conj in range(2):
                    which = 2 * field + conj
                    upper, lower = (im, -im) if conj == 0 else (-im, im)
                    tables[which, parity, part, :h, :h] = re
                    tables[which, parity, part, h:, h:] = re
                    tables[which, parity, part, :h, h:] = upper
                    tables[which, parity, part, h:, :h] = lower

    def fold(part, carry):
        planes = folded([probe_in[part, mode] for mode in range(probe.shape[1])])
        for mode, plane in enumerate(planes):
            probe[part, mode] = plane
        return carry

    lax.fori_loop(0, 2, fold, 0)
    for at, plane in enumerate(folded([measured_in[at] for at in range(measured.shape[0])])):
        measured[at] = plane


def prepared(probe, measured, blocks):
    n = probe.shape[-1]
    return pl.pallas_call(
        prepare_kernel,
        out_shape=(
            jax.ShapeDtypeStruct(probe.shape, F32),
            jax.ShapeDtypeStruct(measured.shape, F32),
            jax.ShapeDtypeStruct((4, 2, 2, n, n), BF),
        ),
        in_specs=[VMEM] * 3,
        out_specs=(VMEM,) * 3,
        compiler_params=pltpu.CompilerParams(vmem_limit_bytes=24 << 20),
        cost_estimate=pl.CostEstimate(flops=3 << 30, bytes_accessed=6 << 20, transcendentals=0),
        name="prepare",
    )(probe, measured, blocks)


def forward_kernel(
    left, left_edges, middle, middle_edges, right, right_edges, probe, tables, phase,
    window, moved, far, intensity, offsets,
    lhs_high, lhs_low, rhs_high, rhs_low, wide, numbers, sems,
):
    n, modes = probe.shape[-1], probe.shape[1]
    rows, tile = wide.shape[2], wide.shape[3] // 3
    pieces = []
    for across, (own, edges) in enumerate(
        ((left, left_edges), (middle, middle_edges), (right, right_edges))
    ):
        sources = (edges.at[:, :, :tile], own, edges.at[:, :, tile + 8 :])
        for down, source in enumerate(sources):
            place = wide.at[
                :, :, down * tile : (down + 1) * tile, across * tile : (across + 1) * tile
            ]
            pieces.append(pltpu.make_async_copy(source, place, sems.at[len(pieces)]))
    pieces.append(
        pltpu.make_async_copy(left_edges.at[:, :, tile : tile + 8], numbers, sems.at[len(pieces)])
    )
    for piece in pieces:
        piece.start()
    for piece in pieces:
        piece.wait()
    for position in range(window.shape[0]):
        for axis in range(2):
            offsets[position, axis] = numbers[position, axis, 0, 0].astype(jnp.int32)
    buffers = (tables, lhs_high, lhs_low, rhs_high, rhs_low)

    def visit(position, carry):
        row, col = offsets[position, 0], offsets[position, 1]
        planes = []
        for layer in range(2):
            for part in range(2):
                plane = pltpu.roll(wide[part, layer], 3 * tile - col, 1)[:, :n]
                planes.append(pltpu.roll(plane, rows - row, 0)[:n])
        planes = folded(planes)
        window[position, 0, 0], window[position, 1, 0] = planes[0], planes[1]
        window[position, 0, 1] = planes[2] * phase[0] - planes[3] * phase[1]
        window[position, 1, 1] = planes[2] * phase[1] + planes[3] * phase[0]

        top_re, top_im = window[position, 0, 0], window[position, 1, 0]
        chains = []
        for mode in range(modes):
            probe_re, probe_im = probe[0, mode], probe[1, mode]
            field = (probe_re * top_re - probe_im * top_im, probe_re * top_im + probe_im * top_re)
            chains.append(sandwich(field, PROP, mode, *buffers))
        low_re, low_im = window[position, 0, 1], window[position, 1, 1]
        following = []
        for mode, (re, im) in enumerate(staggered(chains)):
            moved[position, 0, mode] = re
            moved[position, 1, mode] = im
            field = (re * low_re - im * low_im, re * low_im + im * low_re)
            following.append(sandwich(field, FOUR, mode, *buffers))
        total = jnp.zeros((n, n), F32)
        for mode, (re, im) in enumerate(staggered(following)):
            far[position, 0, mode] = re
            far[position, 1, mode] = im
            total = total + (re * re + im * im)
        intensity[position] = total
        return carry

    lax.fori_loop(0, window.shape[0], visit, 0)


def forward(count, tiles, probe, tables, phase):
    n, modes = probe.shape[-1], probe.shape[1]
    tile = tiles[0].shape[-1]
    fields = jax.ShapeDtypeStruct((count,) + probe.shape, F32)
    return pl.pallas_call(
        forward_kernel,
        out_shape=(
            jax.ShapeDtypeStruct((count, 2, 2, n, n), F32),
            fields,
            fields,
            jax.ShapeDtypeStruct((count, n, n), F32),
            jax.ShapeDtypeStruct((count, 2), jnp.int32),
        ),
        in_specs=[ANY] * 6 + [VMEM] * 3,
        out_specs=(VMEM,) * 4 + (SMEM,),
        scratch_shapes=sandwich_scratch(n, modes)
        + [
            pltpu.VMEM((2, 2, 3 * tile, 3 * tile), F32),
            pltpu.SMEM((2, 2, 8, tile), F32),
            pltpu.SemaphoreType.DMA((10,)),
        ],
        compiler_params=pltpu.CompilerParams(vmem_limit_bytes=SCOPED_F << 20),
        cost_estimate=pl.CostEstimate(
            flops=count * modes * 8 * 12 * n**3, bytes_accessed=18 << 20, transcendentals=0
        ),
        name="forward",
    )(*tiles, probe, tables, phase)


def backward_kernel(
    core, window, moved, far, intensity, measured, probe, tables, phase,
    totals, kept, sent,
    lhs_high, lhs_low, rhs_high, rhs_low, probe_grad, sems,
):
    n, modes = probe.shape[-1], probe.shape[1]
    buffers = (tables, lhs_high, lhs_low, rhs_high, rhs_low)

    def visit(position, carry):
        scaling = 1.0 - measured[position] / jnp.sqrt(intensity[position] + 1.0)

        def chain(mode):
            field = (scaling * far[position, 0, mode], scaling * far[position, 1, mode])
            re, im = yield from sandwich(field, FOUR_CONJ, mode, *buffers)
            moved_re, moved_im = moved[position, 0, mode], moved[position, 1, mode]
            low_terms = (moved_re * re + moved_im * im, moved_re * im - moved_im * re)
            for part in range(2):
                if mode == 0:
                    totals[position, part, 1] = low_terms[part]
                else:
                    totals[position, part, 1] += low_terms[part]
            low_re, low_im = window[position, 0, 1], window[position, 1, 1]
            field = (low_re * re + low_im * im, low_re * im - low_im * re)
            re, im = yield from sandwich(field, PROP_CONJ, mode, *buffers)
            probe_re, probe_im = probe[0, mode], probe[1, mode]
            top_terms = (probe_re * re + probe_im * im, probe_re * im - probe_im * re)
            top_re, top_im = window[position, 0, 0], window[position, 1, 0]
            terms = (top_re * re + top_im * im, top_re * im - top_im * re)
            for part in range(2):
                if mode == 0:
                    totals[position, part, 0] = top_terms[part]
                else:
                    totals[position, part, 0] += top_terms[part]
                before = jnp.where(position == 0, 0.0, probe_grad[part, mode])
                probe_grad[part, mode] = before + terms[part]

        staggered([chain(mode) for mode in range(modes)])
        low_re, low_im = totals[position, 0, 1], totals[position, 1, 1]
        totals[position, 0, 1] = low_re * phase[0] + low_im * phase[1]
        totals[position, 1, 1] = low_im * phase[0] - low_re * phase[1]
        return carry

    lax.fori_loop(0, window.shape[0], visit, 0)

    def unfold(part, carry):
        planes = folded([probe_grad[part, mode] for mode in range(modes)])
        for mode in range(modes):
            probe_grad[part, mode] = planes[mode]
        return carry

    lax.fori_loop(0, 2, unfold, 0)
    copies = [
        pltpu.make_async_copy(probe_grad.at[part], target, sems.at[at])
        for at, (part, target) in enumerate(((core[0], kept), (1 - core[0], sent)))
    ]
    for copy in copies:
        copy.start()
    for copy in copies:
        copy.wait()


def backward(core, state, measured, probe, tables, phase):
    n, modes = probe.shape[-1], probe.shape[1]
    count = measured.shape[0]
    half = jax.ShapeDtypeStruct(probe.shape[1:], F32)
    return pl.pallas_call(
        backward_kernel,
        out_shape=(jax.ShapeDtypeStruct((count, 2, 2, n, n), F32), half, half),
        in_specs=[SMEM] + [VMEM] * 8,
        out_specs=(VMEM, HBM, HBM),
        scratch_shapes=sandwich_scratch(n, modes)
        + [
            pltpu.VMEM(probe.shape, F32),
            pltpu.SemaphoreType.DMA((2,)),
        ],
        compiler_params=pltpu.CompilerParams(vmem_limit_bytes=SCOPED_B << 20),
        cost_estimate=pl.CostEstimate(
            flops=count * modes * 8 * 12 * n**3, bytes_accessed=18 << 20, transcendentals=count * n * n
        ),
        name="backward",
    )(core, *state, measured, probe, tables, phase)


def place_kernel(scalars, totals, grad_left, grad_middle, grad_right, wide, sems):
    n = totals.shape[-1]
    rows, tile = wide.shape[2], wide.shape[3] // 3

    def visit(position, carry):
        row, col = scalars[position, 0], scalars[position, 1]
        at = [(part, layer) for layer in range(2) for part in range(2)]
        planes = folded([totals[position, part, layer] for part, layer in at])
        for (part, layer), plane in zip(at, planes):
            plane = jnp.concatenate([plane, jnp.zeros((rows - n, n), F32)], axis=0)
            plane = pltpu.roll(plane, row, 0)
            plane = jnp.concatenate([plane, jnp.zeros((rows, 3 * tile - n), F32)], axis=1)
            plane = pltpu.roll(plane, col, 1)

            @pl.when(position == 0)
            def _():
                wide[part, layer] = plane

            @pl.when(position != 0)
            def _():
                wide[part, layer] += plane

        return carry

    lax.fori_loop(0, totals.shape[0], visit, 0)
    copies = [
        pltpu.make_async_copy(wide.at[:, :, :, at * tile : (at + 1) * tile], target, sems.at[at])
        for at, target in enumerate((grad_left, grad_middle, grad_right))
    ]
    for copy in copies:
        copy.start()
    for copy in copies:
        copy.wait()


def placed(scalars, totals, rows, tile):
    column = jax.ShapeDtypeStruct((2, 2, rows, tile), F32)
    return pl.pallas_call(
        place_kernel,
        out_shape=(column,) * 3,
        in_specs=[SMEM, VMEM],
        out_specs=(HBM,) * 3,
        scratch_shapes=[pltpu.VMEM((2, 2, rows, 3 * tile), F32), pltpu.SemaphoreType.DMA((3,))],
        compiler_params=pltpu.CompilerParams(vmem_limit_bytes=16 << 20),
        cost_estimate=pl.CostEstimate(flops=2 << 30, bytes_accessed=8 << 20, transcendentals=0),
        name="place",
    )(scalars, totals)


SCOPED_F, SCOPED_B = 20, 20


def around(value, axis, steps):
    count = lax.axis_size(axis)
    return lax.ppermute(value, axis, [(at, (at + steps) % count) for at in range(count)])


def exchanged(value, axis, groups=None):
    return lax.all_to_all(value, axis, 0, 0, tiled=True, axis_index_groups=groups)


def copies(value, count):
    return jnp.broadcast_to(value[None], (count,) + value.shape)


def swapped(value):
    return lax.ppermute(value, "tile", [(at, at ^ 1) for at in range(lax.axis_size("tile"))])


def per_device(object_field, probe_modes, offsets, measured):
    n = probe_modes.shape[-1]
    tile = object_field.shape[2]
    strips, tiles = lax.axis_size("strip"), lax.axis_size("tile")
    both = ("strip", "tile")
    blocks, phase = parity_tables(n)
    phase = jnp.asarray(phase)
    diagonal = [
        (s * tiles + t, (s + 1) % strips * tiles + (t + 1) % tiles)
        for s in range(strips)
        for t in range(tiles)
    ]
    corner = jnp.stack([lax.axis_index("strip"), lax.axis_index("tile")]).astype(jnp.int32) * tile
    local = (offsets - corner).astype(F32)[:, :, None, None]
    sent_down = jnp.concatenate(
        [object_field, jnp.broadcast_to(local, local.shape[:2] + (8, tile))], axis=2
    )
    above = around(sent_down, "strip", 1)
    below = around(object_field, "strip", -1)
    left = around(object_field, "tile", 1)
    right = around(object_field, "tile", -1)
    probe, measured, tables = prepared(probe_modes, measured, jnp.asarray(blocks))
    above, below, left, right = lax.optimization_barrier((above, below, left, right))
    edges = jnp.concatenate([above, below], axis=2)
    left_edges = around(edges, "tile", 1)
    right_edges = around(edges, "tile", -1)
    edges, measured = lax.optimization_barrier((edges, measured))
    measured = lax.ppermute(measured, both, diagonal)
    pieces = (left, left_edges, object_field, edges, right, right_edges)
    *state, scalars = forward(measured.shape[0], pieces, probe, tables, phase)
    core = (lax.axis_index("tile") % 2).astype(jnp.int32)
    totals, kept, sent = backward(core.reshape(1), state, measured, probe, tables, phase)

    cores, pairs = 2, 2
    levels = tiles // cores
    groups = [
        [s * tiles + (pairs * group + at) * cores + c for s in range(strips) for at in range(pairs)]
        for c in range(cores)
        for group in range(levels // pairs)
    ]
    received = swapped(sent)
    grad_left, grad_middle, grad_right = placed(scalars, totals, 3 * tile, tile)
    received, grad_left, grad_middle, grad_right = lax.optimization_barrier(
        (received, grad_left, grad_middle, grad_right)
    )
    from_right = around(grad_left, "tile", -1)
    from_left = around(grad_right, "tile", 1)
    shares = exchanged((kept + received).reshape(strips, -1, n), "strip")
    column = grad_middle + from_right + from_left
    upper, lower = column[:, :, :tile], column[:, :, 2 * tile :]
    from_below = around(upper, "strip", -1)
    from_above = around(lower, "strip", 1)
    shares, column, upper, lower = lax.optimization_barrier((shares, column, upper, lower))

    def across(value, distance):
        step = [
            (z * cores + c, (z ^ distance) * cores + c) for z in range(levels) for c in range(cores)
        ]
        return lax.ppermute(value, "tile", step)

    shares = jnp.sum(shares, axis=0).reshape(pairs, -1, n)
    mine = lax.axis_index("tile") // cores % pairs
    share = lax.dynamic_index_in_dim(shares, mine, 0, False) + across(
        lax.dynamic_index_in_dim(shares, 1 - mine, 0, False), 1
    )
    distance = pairs
    share, from_below, from_above = lax.optimization_barrier((share, from_below, from_above))
    while distance < levels:
        share = share + across(share, distance)
        distance *= 2
    object_grad = column[:, :, tile : 2 * tile] + from_below + from_above
    half = exchanged(copies(share, strips * pairs), both, groups)
    other = swapped(half)
    mine = (jnp.arange(cores) == lax.axis_index("tile") % cores).reshape(cores, 1, 1, 1)
    whole = jnp.where(mine, half[None], other[None])
    return (object_grad, whole.reshape(probe_modes.shape))


def solution(mesh):
    in_specs = (
        P(None, None, "strip", "tile"),
        P(),
        P(("strip", "tile"), None),
        P(("strip", "tile"), None, None),
    )
    out_specs = (P(None, None, "strip", "tile"), P())
    return jax.shard_map(
        per_device, mesh=mesh, in_specs=in_specs, out_specs=out_specs, check_vma=False
    )
```

```python
import jax
import jax.numpy as jnp
import ml_dtypes
import numpy as np
from jax import lax
from jax.experimental import pallas as pl
from jax.experimental.pallas import tpu as pltpu
from jax.sharding import PartitionSpec as P

FRESNEL = 0.5
BF, F32 = jnp.bfloat16, jnp.float32
FOUR, FOUR_CONJ, PROP, PROP_CONJ = 0, 1, 2, 3
STAGGER = 1
VMEM = pl.BlockSpec(memory_space=pltpu.VMEM)
SMEM = pl.BlockSpec(memory_space=pltpu.SMEM)
ANY = pl.BlockSpec(memory_space=pl.ANY)
HBM = pl.BlockSpec(memory_space=pltpu.HBM)


def parity_tables(length):
    half = length // 2
    counter = np.arange(length)
    angles = (counter[:, None] * counter[None, :] % length) * (2 * np.pi / length)
    four = np.exp(-1j * angles) / np.sqrt(length)
    mirrored = np.concatenate([counter[:half], counter[:half - 1:-1]])
    quarter = counter - (length - 1) / 2
    shifted = np.exp(-2j * np.pi * quarter[:, None] * quarter[None, :] / length) / np.sqrt(length)
    centred = (counter + half) % length - half
    kern = np.exp(-1j * np.pi * FRESNEL * centred * centred / length)
    prop = (np.conj(four) * kern[None, :]) @ four
    blocks = []
    for matrix in (shifted, prop):
        folded = matrix[mirrored][:, mirrored]
        same, cross = folded[:half, :half], folded[:half, half:]
        even, odd = (same + cross) / 2, (same - cross) / 2
        for part in ("real", "imag"):
            for block in (even, odd):
                value = getattr(block, part)
                high = value.astype(np.float32).astype(ml_dtypes.bfloat16)
                low = (value - high.astype(np.float64)).astype(np.float32)
                blocks += [high, low.astype(ml_dtypes.bfloat16)]
    turn = np.exp(-2j * np.pi * ((length - 1) / 2) * counter / length)[mirrored]
    phase = turn[:, None] * turn[None, :]
    phase = np.stack([phase.real, phase.imag]).astype(np.float32)
    return np.stack(blocks).reshape(2, 2, 2, 2, half, half), phase


def halves(value):
    high = value.astype(BF)
    return high, (value - high.astype(F32)).astype(BF)


def product(a_high, a_low, b_high, b_low):
    total = jnp.dot(a_high, b_high, preferred_element_type=F32)
    total = total + jnp.dot(a_low, b_high, preferred_element_type=F32)
    return total + jnp.dot(a_high, b_low, preferred_element_type=F32)


def anti_diagonal(h):
    row_at = lax.broadcasted_iota(jnp.int32, (h, h), 0)
    col_at = lax.broadcasted_iota(jnp.int32, (h, h), 1)
    return (row_at + col_at == h - 1).astype(F32).astype(BF)


def folded(planes):
    n = planes[0].shape[0]
    h = n // 2
    anti = anti_diagonal(h)
    flipped = jnp.dot(
        jnp.concatenate([jnp.concatenate(halves(plane[:, h:]), axis=1) for plane in planes], axis=0),
        jnp.concatenate([anti, anti], axis=0),
        preferred_element_type=F32,
    )
    planes = [
        jnp.concatenate([plane[:, :h], flipped[at * n : (at + 1) * n]], axis=1)
        for at, plane in enumerate(planes)
    ]
    flipped = jnp.dot(
        jnp.concatenate([anti, anti], axis=1),
        jnp.concatenate([jnp.concatenate(halves(plane[h:]), axis=0) for plane in planes], axis=1),
        preferred_element_type=F32,
    )
    return [
        jnp.concatenate([plane[:h], flipped[:, at * n : (at + 1) * n]], axis=0)
        for at, plane in enumerate(planes)
    ]


def sandwich(field, which, at, tables, lhs_high, lhs_low, rhs_high, rhs_low):
    n = tables.shape[-1]
    h = n // 2
    rows = slice(at * n, (at + 1) * n)
    for part in range(2):
        first, second = field[part][:, :h], field[part][:, h:]
        for parity, value in enumerate((first + second, first - second)):
            high, low = halves(value)
            lhs_high[parity, rows, part * h : (part + 1) * h] = high
            lhs_low[parity, rows, part * h : (part + 1) * h] = low
    yield
    inner = [
        product(
            lhs_high[parity, rows], lhs_low[parity, rows],
            tables[which, parity, 0], tables[which, parity, 1],
        )
        for parity in range(2)
    ]
    yield
    for parity, value in enumerate(inner):
        first, second = value[:h], value[h:]
        cols = slice(at * n + parity * h, at * n + (parity + 1) * h)
        for turned, mixed in enumerate((first + second, first - second)):
            high, low = halves(mixed)
            rhs_high[turned, :h, cols] = high[:, :h]
            rhs_high[turned, h:, cols] = high[:, h:]
            rhs_low[turned, :h, cols] = low[:, :h]
            rhs_low[turned, h:, cols] = low[:, h:]
    yield
    outer = [
        product(
            tables[which ^ 1, turned, 0], tables[which ^ 1, turned, 1],
            rhs_high[turned, :, rows], rhs_low[turned, :, rows],
        )
        for turned in range(2)
    ]
    yield
    pair = []
    for part in range(2):
        e = outer[0][part * h : (part + 1) * h]
        o = outer[1][part * h : (part + 1) * h]
        value = jnp.concatenate([e + o, e - o], axis=0)
        first, second = value[:, :h], value[:, h:]
        pair.append(jnp.concatenate([first + second, first - second], axis=1))
    return pair


def staggered(chains):
    results = [None] * len(chains)
    running = set(range(len(chains)))
    step = 0
    while running:
        for at in sorted(running):
            if step >= at * STAGGER:
                try:
                    next(chains[at])
                except StopIteration as end:
                    results[at] = end.value
                    running.discard(at)
        step += 1
    return results


def sandwich_scratch(n, modes):
    return [
        pltpu.VMEM((2, modes * n, n), BF),
        pltpu.VMEM((2, modes * n, n), BF),
        pltpu.VMEM((2, n, modes * n), BF),
        pltpu.VMEM((2, n, modes * n), BF),
    ]


def prepare_kernel(probe_in, measured_in, blocks, probe, measured, tables):
    h = blocks.shape[-1]
    for field in range(2):
        for parity in range(2):
            for part in range(2):
                re, im = blocks[field, 0, parity, part], blocks[field, 1, parity, part]
                for conj in range(2):
                    which = 2 * field + conj
                    upper, lower = (im, -im) if conj == 0 else (-im, im)
                    tables[which, parity, part, :h, :h] = re
                    tables[which, parity, part, h:, h:] = re
                    tables[which, parity, part, :h, h:] = upper
                    tables[which, parity, part, h:, :h] = lower

    def fold(part, carry):
        planes = folded([probe_in[part, mode] for mode in range(probe.shape[1])])
        for mode, plane in enumerate(planes):
            probe[part, mode] = plane
        return carry

    lax.fori_loop(0, 2, fold, 0)
    for at, plane in enumerate(folded([measured_in[at] for at in range(measured.shape[0])])):
        measured[at] = plane


def prepared(probe, measured, blocks):
    n = probe.shape[-1]
    return pl.pallas_call(
        prepare_kernel,
        out_shape=(
            jax.ShapeDtypeStruct(probe.shape, F32),
            jax.ShapeDtypeStruct(measured.shape, F32),
            jax.ShapeDtypeStruct((4, 2, 2, n, n), BF),
        ),
        in_specs=[VMEM] * 3,
        out_specs=(VMEM,) * 3,
        compiler_params=pltpu.CompilerParams(vmem_limit_bytes=24 << 20),
        cost_estimate=pl.CostEstimate(flops=3 << 30, bytes_accessed=6 << 20, transcendentals=0),
        name="prepare",
    )(probe, measured, blocks)


def forward_kernel(
    left, left_edges, middle, middle_edges, right, right_edges, probe, tables, phase,
    window, moved, far, intensity, offsets,
    lhs_high, lhs_low, rhs_high, rhs_low, wide, numbers, sems,
):
    n, modes = probe.shape[-1], probe.shape[1]
    rows, tile = wide.shape[2], wide.shape[3] // 3
    pieces = []
    for across, (own, edges) in enumerate(
        ((left, left_edges), (middle, middle_edges), (right, right_edges))
    ):
        sources = (edges.at[:, :, :tile], own, edges.at[:, :, tile + 8 :])
        for down, source in enumerate(sources):
            place = wide.at[
                :, :, down * tile : (down + 1) * tile, across * tile : (across + 1) * tile
            ]
            pieces.append(pltpu.make_async_copy(source, place, sems.at[len(pieces)]))
    pieces.append(
        pltpu.make_async_copy(left_edges.at[:, :, tile : tile + 8], numbers, sems.at[len(pieces)])
    )
    for piece in pieces:
        piece.start()
    for piece in pieces:
        piece.wait()
    for position in range(window.shape[0]):
        for axis in range(2):
            offsets[position, axis] = numbers[position, axis, 0, 0].astype(jnp.int32)
    buffers = (tables, lhs_high, lhs_low, rhs_high, rhs_low)

    def visit(position, carry):
        row, col = offsets[position, 0], offsets[position, 1]
        planes = []
        for layer in range(2):
            for part in range(2):
                plane = pltpu.roll(wide[part, layer], rows - row, 0)[:n]
                planes.append(pltpu.roll(plane, 3 * tile - col, 1)[:, :n])
        planes = folded(planes)
        window[position, 0, 0], window[position, 1, 0] = planes[0], planes[1]
        window[position, 0, 1] = planes[2] * phase[0] - planes[3] * phase[1]
        window[position, 1, 1] = planes[2] * phase[1] + planes[3] * phase[0]

        top_re, top_im = window[position, 0, 0], window[position, 1, 0]
        chains = []
        for mode in range(modes):
            probe_re, probe_im = probe[0, mode], probe[1, mode]
            field = (probe_re * top_re - probe_im * top_im, probe_re * top_im + probe_im * top_re)
            chains.append(sandwich(field, PROP, mode, *buffers))
        low_re, low_im = window[position, 0, 1], window[position, 1, 1]
        following = []
        for mode, (re, im) in enumerate(staggered(chains)):
            moved[position, 0, mode] = re
            moved[position, 1, mode] = im
            field = (re * low_re - im * low_im, re * low_im + im * low_re)
            following.append(sandwich(field, FOUR, mode, *buffers))
        total = jnp.zeros((n, n), F32)
        for mode, (re, im) in enumerate(staggered(following)):
            far[position, 0, mode] = re
            far[position, 1, mode] = im
            total = total + (re * re + im * im)
        intensity[position] = total
        return carry

    lax.fori_loop(0, window.shape[0], visit, 0)


def forward(count, tiles, probe, tables, phase):
    n, modes = probe.shape[-1], probe.shape[1]
    tile = tiles[0].shape[-1]
    fields = jax.ShapeDtypeStruct((count,) + probe.shape, F32)
    return pl.pallas_call(
        forward_kernel,
        out_shape=(
            jax.ShapeDtypeStruct((count, 2, 2, n, n), F32),
            fields,
            fields,
            jax.ShapeDtypeStruct((count, n, n), F32),
            jax.ShapeDtypeStruct((count, 2), jnp.int32),
        ),
        in_specs=[ANY] * 6 + [VMEM] * 3,
        out_specs=(VMEM,) * 4 + (SMEM,),
        scratch_shapes=sandwich_scratch(n, modes)
        + [
            pltpu.VMEM((2, 2, 3 * tile, 3 * tile), F32),
            pltpu.SMEM((2, 2, 8, tile), F32),
            pltpu.SemaphoreType.DMA((10,)),
        ],
        compiler_params=pltpu.CompilerParams(vmem_limit_bytes=SCOPED_F << 20),
        cost_estimate=pl.CostEstimate(
            flops=count * modes * 8 * 12 * n**3, bytes_accessed=18 << 20, transcendentals=0
        ),
        name="forward",
    )(*tiles, probe, tables, phase)


def backward_kernel(
    core, window, moved, far, intensity, measured, probe, tables, phase,
    totals, kept, sent,
    lhs_high, lhs_low, rhs_high, rhs_low, probe_grad, sems,
):
    n, modes = probe.shape[-1], probe.shape[1]
    buffers = (tables, lhs_high, lhs_low, rhs_high, rhs_low)

    def visit(position, carry):
        scaling = 1.0 - measured[position] / jnp.sqrt(intensity[position] + 1.0)

        def chain(mode):
            field = (scaling * far[position, 0, mode], scaling * far[position, 1, mode])
            re, im = yield from sandwich(field, FOUR_CONJ, mode, *buffers)
            moved_re, moved_im = moved[position, 0, mode], moved[position, 1, mode]
            low_terms = (moved_re * re + moved_im * im, moved_re * im - moved_im * re)
            for part in range(2):
                if mode == 0:
                    totals[position, part, 1] = low_terms[part]
                else:
                    totals[position, part, 1] += low_terms[part]
            low_re, low_im = window[position, 0, 1], window[position, 1, 1]
            field = (low_re * re + low_im * im, low_re * im - low_im * re)
            re, im = yield from sandwich(field, PROP_CONJ, mode, *buffers)
            probe_re, probe_im = probe[0, mode], probe[1, mode]
            top_terms = (probe_re * re + probe_im * im, probe_re * im - probe_im * re)
            top_re, top_im = window[position, 0, 0], window[position, 1, 0]
            terms = (top_re * re + top_im * im, top_re * im - top_im * re)
            for part in range(2):
                if mode == 0:
                    totals[position, part, 0] = top_terms[part]
                else:
                    totals[position, part, 0] += top_terms[part]
                before = jnp.where(position == 0, 0.0, probe_grad[part, mode])
                probe_grad[part, mode] = before + terms[part]

        staggered([chain(mode) for mode in range(modes)])
        low_re, low_im = totals[position, 0, 1], totals[position, 1, 1]
        totals[position, 0, 1] = low_re * phase[0] + low_im * phase[1]
        totals[position, 1, 1] = low_im * phase[0] - low_re * phase[1]
        return carry

    lax.fori_loop(0, window.shape[0], visit, 0)

    def unfold(part, carry):
        planes = folded([probe_grad[part, mode] for mode in range(modes)])
        for mode in range(modes):
            probe_grad[part, mode] = planes[mode]
        return carry

    lax.fori_loop(0, 2, unfold, 0)
    copies = [
        pltpu.make_async_copy(probe_grad.at[part], target, sems.at[at])
        for at, (part, target) in enumerate(((core[0], kept), (1 - core[0], sent)))
    ]
    for copy in copies:
        copy.start()
    for copy in copies:
        copy.wait()


def backward(core, state, measured, probe, tables, phase):
    n, modes = probe.shape[-1], probe.shape[1]
    count = measured.shape[0]
    half = jax.ShapeDtypeStruct(probe.shape[1:], F32)
    return pl.pallas_call(
        backward_kernel,
        out_shape=(jax.ShapeDtypeStruct((count, 2, 2, n, n), F32), half, half),
        in_specs=[SMEM] + [VMEM] * 8,
        out_specs=(VMEM, HBM, HBM),
        scratch_shapes=sandwich_scratch(n, modes)
        + [
            pltpu.VMEM(probe.shape, F32),
            pltpu.SemaphoreType.DMA((2,)),
        ],
        compiler_params=pltpu.CompilerParams(vmem_limit_bytes=SCOPED_B << 20),
        cost_estimate=pl.CostEstimate(
            flops=count * modes * 8 * 12 * n**3, bytes_accessed=18 << 20, transcendentals=count * n * n
        ),
        name="backward",
    )(core, *state, measured, probe, tables, phase)


def place_kernel(scalars, totals, grad_left, grad_middle, grad_right, wide, sems):
    n = totals.shape[-1]
    rows, tile = wide.shape[2], wide.shape[3] // 3

    def visit(position, carry):
        row, col = scalars[position, 0], scalars[position, 1]
        at = [(part, layer) for layer in range(2) for part in range(2)]
        planes = folded([totals[position, part, layer] for part, layer in at])
        for (part, layer), plane in zip(at, planes):
            plane = jnp.concatenate([plane, jnp.zeros((n, 3 * tile - n), F32)], axis=1)
            plane = pltpu.roll(plane, col, 1)
            plane = jnp.concatenate([plane, jnp.zeros((rows - n, 3 * tile), F32)], axis=0)
            plane = pltpu.roll(plane, row, 0)

            @pl.when(position == 0)
            def _():
                wide[part, layer] = plane

            @pl.when(position != 0)
            def _():
                wide[part, layer] += plane

        return carry

    lax.fori_loop(0, totals.shape[0], visit, 0)
    copies = [
        pltpu.make_async_copy(wide.at[:, :, :, at * tile : (at + 1) * tile], target, sems.at[at])
        for at, target in enumerate((grad_left, grad_middle, grad_right))
    ]
    for copy in copies:
        copy.start()
    for copy in copies:
        copy.wait()


def placed(scalars, totals, rows, tile):
    column = jax.ShapeDtypeStruct((2, 2, rows, tile), F32)
    return pl.pallas_call(
        place_kernel,
        out_shape=(column,) * 3,
        in_specs=[SMEM, VMEM],
        out_specs=(HBM,) * 3,
        scratch_shapes=[pltpu.VMEM((2, 2, rows, 3 * tile), F32), pltpu.SemaphoreType.DMA((3,))],
        compiler_params=pltpu.CompilerParams(vmem_limit_bytes=16 << 20),
        cost_estimate=pl.CostEstimate(flops=2 << 30, bytes_accessed=8 << 20, transcendentals=0),
        name="place",
    )(scalars, totals)


SCOPED_F, SCOPED_B = 20, 20


def around(value, axis, steps):
    count = lax.axis_size(axis)
    return lax.ppermute(value, axis, [(at, (at + steps) % count) for at in range(count)])


def exchanged(value, axis, groups=None):
    return lax.all_to_all(value, axis, 0, 0, tiled=True, axis_index_groups=groups)


def copies(value, count):
    return jnp.broadcast_to(value[None], (count,) + value.shape)


def swapped(value):
    return lax.ppermute(value, "tile", [(at, at ^ 1) for at in range(lax.axis_size("tile"))])


def per_device(object_field, probe_modes, offsets, measured):
    n = probe_modes.shape[-1]
    tile = object_field.shape[2]
    strips, tiles = lax.axis_size("strip"), lax.axis_size("tile")
    both = ("strip", "tile")
    blocks, phase = parity_tables(n)
    phase = jnp.asarray(phase)
    diagonal = [
        (s * tiles + t, (s + 1) % strips * tiles + (t + 1) % tiles)
        for s in range(strips)
        for t in range(tiles)
    ]
    corner = jnp.stack([lax.axis_index("strip"), lax.axis_index("tile")]).astype(jnp.int32) * tile
    local = (offsets - corner).astype(F32)[:, :, None, None]
    sent_down = jnp.concatenate(
        [object_field, jnp.broadcast_to(local, local.shape[:2] + (8, tile))], axis=2
    )
    above = around(sent_down, "strip", 1)
    below = around(object_field, "strip", -1)
    left = around(object_field, "tile", 1)
    right = around(object_field, "tile", -1)
    probe, measured, tables = prepared(probe_modes, measured, jnp.asarray(blocks))
    above, below, left, right = lax.optimization_barrier((above, below, left, right))
    edges = jnp.concatenate([above, below], axis=2)
    left_edges = around(edges, "tile", 1)
    right_edges = around(edges, "tile", -1)
    edges, measured = lax.optimization_barrier((edges, measured))
    measured = lax.ppermute(measured, both, diagonal)
    pieces = (left, left_edges, object_field, edges, right, right_edges)
    *state, scalars = forward(measured.shape[0], pieces, probe, tables, phase)
    core = (lax.axis_index("tile") % 2).astype(jnp.int32)
    totals, kept, sent = backward(core.reshape(1), state, measured, probe, tables, phase)

    cores, pairs = 2, 2
    levels = tiles // cores
    groups = [
        [s * tiles + (pairs * group + at) * cores + c for s in range(strips) for at in range(pairs)]
        for c in range(cores)
        for group in range(levels // pairs)
    ]
    received = swapped(sent)
    grad_left, grad_middle, grad_right = placed(scalars, totals, 3 * tile, tile)
    received, grad_left, grad_middle, grad_right = lax.optimization_barrier(
        (received, grad_left, grad_middle, grad_right)
    )
    from_right = around(grad_left, "tile", -1)
    from_left = around(grad_right, "tile", 1)
    shares = exchanged((kept + received).reshape(strips, -1, n), "strip")
    column = grad_middle + from_right + from_left
    upper, lower = column[:, :, :tile], column[:, :, 2 * tile :]
    from_below = around(upper, "strip", -1)
    from_above = around(lower, "strip", 1)
    shares, column, upper, lower = lax.optimization_barrier((shares, column, upper, lower))

    def across(value, distance):
        step = [
            (z * cores + c, (z ^ distance) * cores + c) for z in range(levels) for c in range(cores)
        ]
        return lax.ppermute(value, "tile", step)

    shares = jnp.sum(shares, axis=0).reshape(pairs, -1, n)
    mine = lax.axis_index("tile") // cores % pairs
    share = lax.dynamic_index_in_dim(shares, mine, 0, False) + across(
        lax.dynamic_index_in_dim(shares, 1 - mine, 0, False), 1
    )
    distance = pairs
    share, from_below, from_above = lax.optimization_barrier((share, from_below, from_above))
    while distance < levels:
        share = share + across(share, distance)
        distance *= 2
    object_grad = column[:, :, tile : 2 * tile] + from_below + from_above
    half = exchanged(copies(share, strips * pairs), both, groups)
    other = swapped(half)
    mine = (jnp.arange(cores) == lax.axis_index("tile") % cores).reshape(cores, 1, 1, 1)
    whole = jnp.where(mine, half[None], other[None])
    return (object_grad, whole.reshape(probe_modes.shape))


def solution(mesh):
    in_specs = (
        P(None, None, "strip", "tile"),
        P(),
        P(("strip", "tile"), None),
        P(("strip", "tile"), None, None),
    )
    out_specs = (P(None, None, "strip", "tile"), P())
    return jax.shard_map(
        per_device, mesh=mesh, in_specs=in_specs, out_specs=out_specs, check_vma=False
    )
```
